32 devices in a mesh: dp: 16 (over z, x, core), mp: 2 (over y).
Axes of the slice: x: 2, y: 2, z: 4, core: 2. Of those that a mesh axis runs over, the one named last changes fastest.
Arguments:
- latents: bfloat16 [16, 16, 32, 1152], P('dp'), may hold values from -6 to 6
- conditioning: float32 [16, 1152], P('dp'), may hold values from -6 to 6
- clip_mask: int32 [16], P('dp'), may hold values 0 or 1
- qkv_weight: bfloat16 [1152, 3, 1152], P(None, None, 'mp'), may hold values from -0.25 to 0.25
- qv_bias: bfloat16 [2, 1152], P(None, 'mp'), may hold values from -3 to 3
- proj_weight: bfloat16 [1152, 1152], P('mp'), may hold values from -0.375 to 0.375
- proj_bias: bfloat16 [1152], replicated, may hold values from -3 to 3
- fc1_weight: bfloat16 [1152, 4608], P(None, 'mp'), may hold values from -0.1875 to 0.1875
- fc1_bias: bfloat16 [4608], P('mp'), may hold values from -3 to 3
- fc2_weight: bfloat16 [4608, 1152], P('mp'), may hold values from -0.125 to 0.125
- fc2_bias: bfloat16 [1152], replicated, may hold values from -3 to 3
- ada_weight: bfloat16 [1152, 6912], P(None, 'mp'), may hold values from -0.1875 to 0.1875
- ada_bias: bfloat16 [6912], P('mp'), may hold values from -3 to 3
- out_cotangent: bfloat16 [16, 16, 32, 1152], P('dp'), may hold values from -6 to 6
Outputs:
- output: float32 [16, 16, 32, 1152], P('dp')
- latents_grad: float32 [16, 16, 32, 1152], P('dp')
- conditioning_grad: float32 [16, 1152], P('dp')
- qkv_weight_grad: float32 [1152, 3, 1152], P('dp', None, 'mp')
- qv_bias_grad: float32 [2, 1152], P(None, 'mp')
- proj_weight_grad: float32 [1152, 1152], P('mp', 'dp')
- proj_bias_grad: float32 [1152], replicated
- fc1_weight_grad: float32 [1152, 4608], P('dp', 'mp')
- fc1_bias_grad: float32 [4608], P('mp')
- fc2_weight_grad: float32 [4608, 1152], P('mp', 'dp')
- fc2_bias_grad: float32 [1152], replicated
- ada_weight_grad: float32 [1152, 6912], P('dp', 'mp')
- ada_bias_grad: float32 [6912], P('mp')
The draws below stay inside these ranges and needn't reach their ends.
All inputs are finite; a program needn't handle non-finite values. No bound on the sum of `clip_mask` on one device may be relied on, other than what follows from the above.
Results may differ from the reference program's by a relative error of at most 0.02.
The reference program's roundings to bfloat16 on the way count: a program that leaves them out, or rounds other values in their place, can miss the bound.
Values may be sent and summed in bfloat16 or wider, within the bound.
A program may use at most 128 MiB of HBM per device.

```python
import jax
import jax.numpy as jnp
from jax import lax

D = 1152
HEADS = 16
HEAD_DIM = 72
FF = 4608
FRAMES = 16
PATCHES = 32
ITEMS = 16


def touch_ends(entries, stream_key, smallest, largest):
    index_at = [jax.random.randint(jax.random.fold_in(stream_key, axis), (), 0, length) for axis, length in enumerate(entries.shape)]
    main_axis = entries.shape.index(max(entries.shape))
    next_to = index_at[:main_axis] + [(index_at[main_axis] + 1) % entries.shape[main_axis]] + index_at[main_axis + 1:]
    return entries.at[tuple(index_at)].set(smallest).at[tuple(next_to)].set(largest)


def level_of(key, shape, shards, low, high):
    loudness = 1.0
    for axis_at, shards_of in shards:
        steps = jax.random.uniform(jax.random.fold_in(jax.random.fold_in(key, 6), axis_at), (shards_of,), jnp.float32, low / len(shards), high / len(shards))
        loudness = loudness * jnp.repeat(jnp.exp(steps), shape[axis_at] // shards_of).reshape((-1,) + (1,) * (len(shape) - 1 - axis_at))
    return loudness


def scatter_about(stream_key, dims, deviation, limit, cuts=(), held_as=jnp.bfloat16):
    gain = level_of(stream_key, dims, cuts, -0.22, 0.18) if cuts else 1.0
    result = jax.random.normal(stream_key, dims, jnp.float32) * deviation * gain
    return jnp.minimum(jnp.maximum(result, -limit), limit).astype(held_as)


def setup_inputs(seed: int = 0) -> dict:
    key_of = jax.random.split(jax.random.key(seed), 15)
    return {
        "latents": scatter_about(key_of[0], (ITEMS, FRAMES, PATCHES, D), 1.0, 6.0, ((0, 16),)),
        "conditioning": scatter_about(key_of[1], (ITEMS, D), 1.0, 6.0, ((0, 16),), jnp.float32),
        "clip_mask": touch_ends((jax.random.randint(key_of[2], (ITEMS,), 0, 38) < 22).astype(jnp.int32), jax.random.fold_in(key_of[2], 1), 0, 1),
        "qkv_weight": scatter_about(key_of[3], (D, 3, D), (D // 2) ** -0.5, 0.25, ((2, 2),)),
        "qv_bias": scatter_about(key_of[4], (2, D), 0.5, 3.0, ((1, 2),)),
        "proj_weight": scatter_about(key_of[5], (D, D), (D // 4) ** -0.5, 0.375, ((0, 2),)),
        "proj_bias": scatter_about(key_of[6], (D,), 0.5, 3.0),
        "fc1_weight": scatter_about(key_of[7], (D, FF), D ** -0.5, 0.1875, ((1, 2),)),
        "fc1_bias": scatter_about(key_of[8], (FF,), 0.5, 3.0, ((0, 2),)),
        "fc2_weight": scatter_about(key_of[9], (FF, D), (FF // 2) ** -0.5, 0.125, ((0, 2),)),
        "fc2_bias": scatter_about(key_of[10], (D,), 0.5, 3.0),
        "ada_weight": scatter_about(key_of[11], (D, 6 * D), D ** -0.5, 0.1875, ((1, 2),)),
        "ada_bias": scatter_about(key_of[12], (6 * D,), 0.5, 3.0, ((0, 2),)),
        "out_cotangent": scatter_about(key_of[13], (ITEMS, FRAMES, PATCHES, D), 1.0, 6.0, ((0, 16),)),
    }


@jax.custom_vjp
def low(v):
    return lax.optimization_barrier(v.astype(jnp.bfloat16)).astype(jnp.float32)

@jax.custom_vjp
def low_back(v):
    return v

def low_keep(v):
    return (low(v), None)

def low_pass(kept, grad):
    return (grad,)

def back_keep(v):
    return (v, None)

def back_low(kept, grad):
    return (low(grad),)
low.defvjp(low_keep, low_pass)
low_back.defvjp(back_keep, back_low)

def normalize(values):
    centered = values - lax.optimization_barrier(jnp.mean(values, axis=-1, keepdims=True))
    return centered * lax.rsqrt(lax.optimization_barrier(jnp.mean(centered * centered, axis=-1, keepdims=True)) + 1e-06)

def attend(block):
    query, keys, values = block
    highest = lax.Precision.HIGHEST
    scores = jnp.einsum('fphd,gphd->phfg', query, keys, precision=highest) * HEAD_DIM ** (-0.5)
    scores = low_back(scores)
    weights = jax.nn.softmax(scores, axis=-1)
    mixed = jnp.einsum('phfg,gphd->fphd', low(weights), values, precision=highest)
    return low_back(low(mixed))

def forward(latents, conditioning, qkv_weight, qv_bias, proj_weight, proj_bias, fc1_weight, fc1_bias, fc2_weight, fc2_bias, ada_weight, ada_bias, mask_value):
    highest = lax.Precision.HIGHEST
    scaled = low(jax.nn.silu(conditioning))
    modulation = low_back(jnp.dot(scaled, ada_weight, precision=highest)) + ada_bias
    pieces = modulation.reshape(ITEMS, 6, 1, 1, D)
    shift_one = pieces[:, 0]
    scale_one = pieces[:, 1]
    gate_one = pieces[:, 2]
    shift_two = pieces[:, 3]
    scale_two = pieces[:, 4]
    gate_two = pieces[:, 5]
    normed_one = normalize(latents)
    entry_one = low(normed_one * (1.0 + scale_one) + shift_one)
    projected = jnp.dot(entry_one.reshape(-1, D), qkv_weight.reshape(D, 3 * D), precision=highest)
    bias_full = jnp.stack([qv_bias[0], jnp.zeros_like(qv_bias[0]), qv_bias[1]]).reshape(3 * D)
    projected = low_back(low(projected + bias_full)).reshape(ITEMS, FRAMES, PATCHES, 3, HEADS, HEAD_DIM)
    mixed = lax.map(jax.checkpoint(attend), (projected[:, :, :, 0], projected[:, :, :, 1], projected[:, :, :, 2]))
    attention = low_back(jnp.dot(mixed.reshape(-1, D), proj_weight, precision=highest)).reshape(latents.shape) + proj_bias
    middle = latents + mask_value[:, None, None, None] * gate_one * attention
    normed_two = normalize(middle)
    entry_two = low(normed_two * (1.0 + scale_two) + shift_two)
    hidden = low_back(jnp.dot(entry_two.reshape(-1, D), fc1_weight, precision=highest)) + fc1_bias
    activated = low(jax.nn.gelu(hidden, approximate=True))
    branch = low_back(jnp.dot(activated, fc2_weight, precision=highest)).reshape(latents.shape) + fc2_bias
    return middle + gate_two * branch

def reference(latents, conditioning, clip_mask, qkv_weight, qv_bias, proj_weight, proj_bias, fc1_weight, fc1_bias, fc2_weight, fc2_bias, ada_weight, ada_bias, out_cotangent):
    mask_value = clip_mask.astype(jnp.float32)
    floats = [latents, conditioning, qkv_weight, qv_bias, proj_weight, proj_bias, fc1_weight, fc1_bias, fc2_weight, fc2_bias, ada_weight, ada_bias]
    floats = [item.astype(jnp.float32) for item in floats]

    def wrapped(*params):
        return forward(*params, mask_value)
    output, pullback = jax.vjp(wrapped, *floats)
    grads = pullback(out_cotangent.astype(jnp.float32))
    return (output, grads[0], grads[1], grads[2], grads[3], grads[4], grads[5], grads[6], grads[7], grads[8], grads[9], grads[10], grads[11])
```

```python
from functools import partial

import jax
import jax.numpy as jnp
from jax import lax
from jax.experimental import pallas as pl
from jax.experimental.pallas import tpu as pltpu
from jax.sharding import PartitionSpec as P

HEAD_DIM = 72


def normalize(values):
    centered = values - jnp.mean(values, axis=-1, keepdims=True)
    inverse = lax.rsqrt(jnp.mean(centered * centered, axis=-1, keepdims=True) + 1e-06)
    return (centered * inverse, inverse)


def norm_back(grad_normed, normed, inverse):
    first = jnp.mean(grad_normed, axis=-1, keepdims=True)
    second = jnp.mean(grad_normed * normed, axis=-1, keepdims=True)
    return inverse * (grad_normed - first - normed * second)


def general_body(
    latents,
    conditioning,
    clip_mask,
    qkv_weight,
    qv_bias,
    proj_weight,
    proj_bias,
    fc1_weight,
    fc1_bias,
    fc2_weight,
    fc2_bias,
    ada_weight,
    ada_bias,
    out_cotangent,
):
    frames = latents.shape[1]
    patches = latents.shape[2]
    width = latents.shape[3]
    tok_count = frames * patches
    local_width = qkv_weight.shape[2]
    local_heads = local_width // HEAD_DIM
    factor = HEAD_DIM ** (-0.5)
    stream = latents.reshape(tok_count, width).astype(jnp.float32)
    scaled = jax.nn.silu(conditioning)
    scaled_low = scaled.astype(jnp.bfloat16)
    mod_local = jnp.dot(
        scaled_low, ada_weight, preferred_element_type=jnp.float32
    ) + ada_bias.astype(jnp.float32)
    modulation = lax.all_gather(mod_local, "mp", axis=1, tiled=True).reshape(6, width)
    shift_one = modulation[0]
    scale_one = modulation[1]
    gate_one = modulation[2]
    shift_two = modulation[3]
    scale_two = modulation[4]
    gate_two = modulation[5]
    is_clip = clip_mask[0] > 0
    mask_value = clip_mask[0].astype(jnp.float32)
    normed_one, inverse_one = normalize(stream)
    entry_one = (normed_one * (1.0 + scale_one) + shift_one).astype(jnp.bfloat16)
    qkv_flat = qkv_weight.reshape(width, 3 * local_width)
    bias_rows = qv_bias.astype(jnp.float32)
    bias_full = jnp.stack([bias_rows[0], jnp.zeros_like(bias_rows[0]), bias_rows[1]]).reshape(
        3 * local_width
    )

    def split_heads(projected):
        parts = projected.reshape(frames, patches, 3, local_heads, HEAD_DIM)
        return (parts[:, :, 0], parts[:, :, 1], parts[:, :, 2])

    def softmax_weights(query, keys):
        scores = (
            jnp.einsum("fphd,gphd->phfg", query, keys, preferred_element_type=jnp.float32) * factor
        )
        return jax.nn.softmax(scores, axis=-1)

    def attn_forward(entry):
        projected = (
            jnp.dot(entry, qkv_flat, preferred_element_type=jnp.float32) + bias_full
        ).astype(jnp.bfloat16)
        query, keys, values = split_heads(projected)
        weights = softmax_weights(query, keys)
        mixed = jnp.einsum(
            "phfg,gphd->fphd",
            weights.astype(jnp.bfloat16),
            values,
            preferred_element_type=jnp.float32,
        )
        mixed = mixed.astype(jnp.bfloat16).reshape(tok_count, local_width)
        partial_out = jnp.dot(mixed, proj_weight, preferred_element_type=jnp.float32)
        return (partial_out, projected, mixed)

    def attn_skip(entry):
        return (
            jnp.zeros((tok_count, width), jnp.float32),
            jnp.zeros((tok_count, 3 * local_width), jnp.bfloat16),
            jnp.zeros((tok_count, local_width), jnp.bfloat16),
        )

    partial_out, projected, mixed = lax.cond(is_clip, attn_forward, attn_skip, entry_one)
    attention = lax.psum(partial_out.astype(jnp.bfloat16), "mp").astype(
        jnp.float32
    ) + proj_bias.astype(jnp.float32)
    middle = stream + mask_value * gate_one * attention
    normed_two, inverse_two = normalize(middle)
    entry_two = (normed_two * (1.0 + scale_two) + shift_two).astype(jnp.bfloat16)
    hidden = jnp.dot(entry_two, fc1_weight, preferred_element_type=jnp.float32) + fc1_bias.astype(
        jnp.float32
    )
    activated = jax.nn.gelu(hidden, approximate=True).astype(jnp.bfloat16)
    branch_part = jnp.dot(activated, fc2_weight, preferred_element_type=jnp.float32)
    branch = lax.psum(branch_part.astype(jnp.bfloat16), "mp").astype(jnp.float32) + fc2_bias.astype(
        jnp.float32
    )
    output = middle + gate_two * branch
    grad_out = out_cotangent.reshape(tok_count, width).astype(jnp.float32)
    grad_branch = gate_two * grad_out
    grad_fc2_bias = jnp.sum(grad_branch, axis=0)
    branch_low = grad_branch.astype(jnp.bfloat16)
    grad_fc2 = jnp.einsum("ti,tj->ij", activated, branch_low, preferred_element_type=jnp.float32)
    grad_act = jnp.einsum("tj,ij->ti", branch_low, fc2_weight, preferred_element_type=jnp.float32)
    grad_hidden = jax.vjp(partial(jax.nn.gelu, approximate=True), hidden)[1](grad_act)[0]
    grad_fc1_bias = jnp.sum(grad_hidden, axis=0)
    hidden_low = grad_hidden.astype(jnp.bfloat16)
    grad_fc1 = jnp.einsum("ti,tj->ij", entry_two, hidden_low, preferred_element_type=jnp.float32)
    entry_two_part = jnp.einsum(
        "tj,ij->ti", hidden_low, fc1_weight, preferred_element_type=jnp.float32
    )
    grad_entry_two = lax.psum(entry_two_part.astype(jnp.bfloat16), "mp").astype(jnp.float32)
    grad_gate_two = jnp.sum(grad_out * branch, axis=0)
    grad_shift_two = jnp.sum(grad_entry_two, axis=0)
    grad_scale_two = jnp.sum(grad_entry_two * normed_two, axis=0)
    grad_middle = grad_out + norm_back(grad_entry_two * (1.0 + scale_two), normed_two, inverse_two)
    grad_gate_one = mask_value * jnp.sum(grad_middle * attention, axis=0)
    grad_attention = mask_value * gate_one * grad_middle
    grad_proj_bias = jnp.sum(grad_attention, axis=0)
    attention_low = grad_attention.astype(jnp.bfloat16)

    def attn_backward(operands):
        grad_low, kept_projected, kept_mixed = operands
        grad_proj = jnp.einsum(
            "ti,tj->ij", kept_mixed, grad_low, preferred_element_type=jnp.float32
        )
        grad_mixed = jnp.einsum(
            "tj,ij->ti", grad_low, proj_weight, preferred_element_type=jnp.float32
        )
        grad_mixed = grad_mixed.astype(jnp.bfloat16).reshape(frames, patches, local_heads, HEAD_DIM)
        query, keys, values = split_heads(kept_projected)
        weights = softmax_weights(query, keys)
        grad_values = jnp.einsum(
            "phfg,fphd->gphd",
            weights.astype(jnp.bfloat16),
            grad_mixed,
            preferred_element_type=jnp.float32,
        )
        grad_weights = jnp.einsum(
            "fphd,gphd->phfg", grad_mixed, values, preferred_element_type=jnp.float32
        )
        grad_scores = weights * (
            grad_weights - jnp.sum(weights * grad_weights, axis=-1, keepdims=True)
        )
        grad_scores = grad_scores.astype(jnp.bfloat16)
        grad_query = (
            jnp.einsum("phfg,gphd->fphd", grad_scores, keys, preferred_element_type=jnp.float32)
            * factor
        )
        grad_keys = (
            jnp.einsum("phfg,fphd->gphd", grad_scores, query, preferred_element_type=jnp.float32)
            * factor
        )
        grad_all = (
            jnp.stack([grad_query, grad_keys, grad_values], axis=2)
            .astype(jnp.bfloat16)
            .reshape(tok_count, 3 * local_width)
        )
        column_sums = jnp.sum(grad_all.astype(jnp.float32), axis=0).reshape(3, local_width)
        grad_qv = jnp.stack([column_sums[0], column_sums[2]])
        grad_qkv = jnp.einsum(
            "ti,tj->ij", entry_one, grad_all, preferred_element_type=jnp.float32
        ).reshape(width, 3, local_width)
        grad_entry = jnp.einsum("tj,ij->ti", grad_all, qkv_flat, preferred_element_type=jnp.float32)
        return (grad_proj, grad_qv, grad_qkv, grad_entry)

    def skip_backward(operands):
        return (
            jnp.zeros((local_width, width), jnp.float32),
            jnp.zeros((2, local_width), jnp.float32),
            jnp.zeros((width, 3, local_width), jnp.float32),
            jnp.zeros((tok_count, width), jnp.float32),
        )

    grad_proj, grad_qv, grad_qkv, entry_one_part = lax.cond(
        is_clip, attn_backward, skip_backward, (attention_low, projected, mixed)
    )
    grad_entry_one = lax.psum(entry_one_part.astype(jnp.bfloat16), "mp").astype(jnp.float32)
    grad_shift_one = jnp.sum(grad_entry_one, axis=0)
    grad_scale_one = jnp.sum(grad_entry_one * normed_one, axis=0)
    grad_latents = grad_middle + norm_back(
        grad_entry_one * (1.0 + scale_one), normed_one, inverse_one
    )
    grad_modulation = jnp.concatenate(
        [
            grad_shift_one,
            grad_scale_one,
            grad_gate_one,
            grad_shift_two,
            grad_scale_two,
            grad_gate_two,
        ]
    )
    local_cols = ada_weight.shape[1]
    grad_mod_local = lax.dynamic_slice_in_dim(
        grad_modulation, lax.axis_index("mp") * local_cols, local_cols
    )[None, :]
    grad_ada_bias = jnp.sum(grad_mod_local, axis=0)
    modulation_low = grad_mod_local.astype(jnp.bfloat16)
    scaled_part = jnp.einsum(
        "tj,ij->ti", modulation_low, ada_weight, preferred_element_type=jnp.float32
    )
    grad_scaled = lax.psum(scaled_part, "mp")
    grad_cond = jax.vjp(jax.nn.silu, conditioning)[1](grad_scaled)[0]
    ada_term = jnp.einsum(
        "ti,tj->ij", scaled_low, modulation_low, preferred_element_type=jnp.float32
    )
    grad_ada = lax.psum_scatter(
        ada_term.astype(jnp.bfloat16), "dp", scatter_dimension=0, tiled=True
    ).astype(jnp.float32)
    qkv_total, proj_total, fc1_total, fc2_total = (
        lax.psum_scatter(
            grad_qkv.astype(jnp.bfloat16), "dp", scatter_dimension=0, tiled=True
        ).astype(jnp.float32),
        lax.psum_scatter(
            grad_proj.astype(jnp.bfloat16), "dp", scatter_dimension=1, tiled=True
        ).astype(jnp.float32),
        lax.psum_scatter(
            grad_fc1.astype(jnp.bfloat16), "dp", scatter_dimension=0, tiled=True
        ).astype(jnp.float32),
        lax.psum_scatter(
            grad_fc2.astype(jnp.bfloat16), "dp", scatter_dimension=1, tiled=True
        ).astype(jnp.float32),
    )
    qv_total, proj_bias_total, fc1_bias_total, fc2_bias_total, ada_bias_total = lax.psum(
        (grad_qv, grad_proj_bias, grad_fc1_bias, grad_fc2_bias, grad_ada_bias), "dp"
    )
    return (
        output.reshape(latents.shape),
        grad_latents.reshape(latents.shape),
        grad_cond,
        qkv_total,
        qv_total,
        proj_total,
        proj_bias_total,
        fc1_total,
        fc1_bias_total,
        fc2_total,
        fc2_bias_total,
        grad_ada,
        ada_bias_total,
    )


NT = (((1,), (1,)), ((), ()))
TN = (((0,), (0,)), ((), ()))
CHUNKS = 2
GELU_A = 0.7978845608028654
GELU_B = 0.044715
VMEM = pl.BlockSpec(memory_space=pltpu.VMEM)
ANY = pl.BlockSpec(memory_space=pl.ANY)
SMEM = pl.BlockSpec(memory_space=pltpu.SMEM)


def params(mib):
    return pltpu.CompilerParams(vmem_limit_bytes=mib << 20)


def cost(flops, nbytes):
    return pl.CostEstimate(flops=int(flops), bytes_accessed=int(nbytes), transcendentals=0)


def f32(values):
    return values.astype(jnp.float32)


def bf16(values):
    return values.astype(jnp.bfloat16)


def dot(left, right, dims=(((1,), (0,)), ((), ()))):
    return lax.dot_general(left, right, dims, preferred_element_type=jnp.float32)


def over_rows(rows, step, visit):
    def at(i, carry):
        visit(pl.multiple_of(i * step, step))
        return carry

    lax.fori_loop(0, rows // step, at, 0)


def token_rows(ref, row, step, per_frame):
    frame = row // per_frame
    block = ref[0, pl.ds(frame, step // per_frame), :, :]
    return f32(block).reshape(step, ref.shape[-1])


def head_spans(width):
    spans = []
    for head in range(width // HEAD_DIM):
        first, last = head * HEAD_DIM, (head + 1) * HEAD_DIM
        low = first // 128 * 128
        high = min(-(-last // 128) * 128, width)
        spans.append((first, last, low, high))
    return spans


def lane_mask(first, last, low, high):
    lane = lax.broadcasted_iota(jnp.int32, (1, high - low), 1) + low
    return (lane >= first) & (lane < last)


def same_patch(tokens, per_frame):
    row = lax.broadcasted_iota(jnp.int32, (tokens, tokens), 0)
    col = lax.broadcasted_iota(jnp.int32, (tokens, tokens), 1)
    return (row % per_frame) == (col % per_frame)


def attention_weights(query, keys, allowed):
    scores = dot(query, keys, NT) * (HEAD_DIM ** (-0.5))
    scores = jnp.where(allowed, scores, -1e30)
    grown = jnp.exp(scores - jnp.max(scores, axis=-1, keepdims=True))
    return grown / jnp.sum(grown, axis=-1, keepdims=True)


def start_pieces(pairs, sems):
    copies = [
        pltpu.make_async_copy(source, target, sems.at[i]) for i, (source, target) in enumerate(pairs)
    ]
    for copy in copies:
        copy.start()
    return copies


def first_kernel(
    lat_ref, vec_ref, bias_ref, w_hbm, pw_hbm, part_ref, proj_ref, mixed_ref, entry_ref, w_v, pw_v, sems
):
    tokens, width = part_ref.shape
    local = mixed_ref.shape[1]
    per_frame = lat_ref.shape[2]
    copies = start_pieces([(w_hbm.at[s], w_v.at[s]) for s in range(3)] + [(pw_hbm, pw_v)], sems)
    step = 2 * per_frame

    def enter(row):
        values = token_rows(lat_ref, row, step, per_frame)
        normed, _ = normalize(values)
        entry_ref[pl.ds(row, step), :] = bf16(normed * vec_ref[1:2, :] + vec_ref[0:1, :])

    over_rows(tokens, step, enter)
    for s in range(3):
        copies[s].wait()
        proj_ref[s] = bf16(dot(entry_ref[...], w_v[s], NT) + bias_ref[s : s + 1, :])
    allowed = same_patch(tokens, per_frame)
    for first, last, low, high in head_spans(local):
        mask = lane_mask(first, last, low, high)
        query = jnp.where(mask, proj_ref[0, :, low:high], 0)
        weights = attention_weights(query, proj_ref[1, :, low:high], allowed)
        mixed = dot(bf16(weights), proj_ref[2, :, low:high])
        mixed_ref[:, low:high] = bf16(jnp.where(mask, mixed, f32(mixed_ref[:, low:high])))
    copies[3].wait()
    part_ref[...] = bf16(dot(mixed_ref[...], pw_v[...]))


def middle_rows(own_ref, recv_ref, lat_ref, vec_ref, row, step, per_frame):
    at = pl.ds(row, step)
    attention = f32(own_ref[at, :]) + f32(recv_ref[at, :]) + vec_ref[6:7, :]
    values = token_rows(lat_ref, row, step, per_frame)
    return attention, values + vec_ref[2:3, :] * attention


def second_kernel(
    own_ref,
    recv_ref,
    lat_ref,
    vec_ref,
    b1_ref,
    ga_ref,
    w1_hbm,
    part_ref,
    entry_ref,
    act_ref,
    low_ref,
    sums_ref,
    w1_v,
    sems,
):
    tokens, width = part_ref.shape
    hidden_width = act_ref.shape[1]
    per_frame = lat_ref.shape[2]
    pieces = 3
    piece = hidden_width // pieces
    copies = start_pieces(
        [
            (w1_hbm.at[:, i * piece : (i + 1) * piece], w1_v.at[:, i * piece : (i + 1) * piece])
            for i in range(pieces)
        ],
        sems,
    )
    step = 2 * per_frame

    def enter(row):
        _, middle = middle_rows(own_ref, recv_ref, lat_ref, vec_ref, row, step, per_frame)
        normed, _ = normalize(middle)
        entry_ref[pl.ds(row, step), :] = bf16(normed * vec_ref[4:5, :] + vec_ref[3:4, :])

    over_rows(tokens, step, enter)
    tile = 256 if piece % 256 == 0 else piece

    def columns(col):
        at = pl.ds(col, tile)
        hidden = dot(entry_ref[...], w1_v[:, at]) + b1_ref[:, at]
        square = hidden * hidden
        bent = jnp.tanh(GELU_A * hidden * (1.0 + GELU_B * square))
        half = 0.5 * (1.0 + bent)
        act_ref[:, at] = bf16(hidden * half)
        slope = half + 0.5 * hidden * (1.0 - bent * bent) * (
            GELU_A * (1.0 + 3.0 * GELU_B * square)
        )
        grad_hidden = f32(ga_ref[:, at]) * slope
        sums_ref[:, at] = jnp.sum(grad_hidden, axis=0, keepdims=True)
        low_ref[:, at] = bf16(grad_hidden)

    for i in range(pieces):
        copies[i].wait()

        def at(j, carry, i=i):
            columns(pl.multiple_of(i * piece + j * tile, tile))
            return carry

        lax.fori_loop(0, piece // tile, at, 0)
    rows = width // 3

    def back(row):
        part_ref[:, pl.ds(row, rows)] = bf16(dot(low_ref[...], w1_v[pl.ds(row, rows), :], NT))

    over_rows(width, rows, back)


def third_kernel(
    own_ref,
    recv_ref,
    own2_ref,
    recv2_ref,
    lat_ref,
    dy_ref,
    vec_ref,
    proj_ref,
    w_hbm,
    pw_hbm,
    part_ref,
    gproj_ref,
    alow_ref,
    gmid_ref,
    stat_ref,
    qsum_ref,
    w_v,
    pw_v,
    gm_v,
    sems,
):
    tokens, width = part_ref.shape
    local = gm_v.shape[1]
    per_frame = lat_ref.shape[2]
    copies = start_pieces([(pw_hbm, pw_v)] + [(w_hbm.at[s], w_v.at[s]) for s in range(3)], sems)
    step = 2 * per_frame
    stat_ref[...] = jnp.zeros_like(stat_ref)

    def enter(row):
        at = pl.ds(row, step)
        attention, middle = middle_rows(own_ref, recv_ref, lat_ref, vec_ref, row, step, per_frame)
        normed, inverse = normalize(middle)
        grad_entry = f32(own2_ref[at, :]) + f32(recv2_ref[at, :])
        stat_ref[0:1, :] += jnp.sum(grad_entry, axis=0, keepdims=True)
        stat_ref[1:2, :] += jnp.sum(grad_entry * normed, axis=0, keepdims=True)
        grad_middle = token_rows(dy_ref, row, step, per_frame) + norm_back(
            grad_entry * vec_ref[4:5, :], normed, inverse
        )
        stat_ref[2:3, :] += jnp.sum(grad_middle * attention, axis=0, keepdims=True)
        stat_ref[3:4, :] += jnp.sum(grad_middle, axis=0, keepdims=True)
        gmid_ref[at, :] = grad_middle
        alow_ref[at, :] = bf16(vec_ref[2:3, :] * grad_middle)

    over_rows(tokens, step, enter)
    copies[0].wait()
    gm_v[...] = bf16(dot(alow_ref[...], pw_v[...], NT))
    allowed = same_patch(tokens, per_frame)
    factor = HEAD_DIM ** (-0.5)
    for first, last, low, high in head_spans(local):
        mask = lane_mask(first, last, low, high)
        query, keys, values = (proj_ref[s, :, low:high] for s in range(3))
        grad_mixed = gm_v[:, low:high]
        weights = attention_weights(jnp.where(mask, query, 0), keys, allowed)
        grad_weights = dot(jnp.where(mask, grad_mixed, 0), values, NT)
        grad_scores = weights * (
            grad_weights - jnp.sum(weights * grad_weights, axis=-1, keepdims=True)
        )
        grad_scores = bf16(grad_scores)
        found = (
            dot(grad_scores, keys) * factor,
            dot(grad_scores, query, TN) * factor,
            dot(bf16(weights), grad_mixed, TN),
        )
        for s in range(3):
            gproj_ref[s, :, low:high] = bf16(
                jnp.where(mask, found[s], f32(gproj_ref[s, :, low:high]))
            )
    for s in range(3):
        copies[s + 1].wait()
        qsum_ref[s : s + 1, :] = jnp.sum(f32(gproj_ref[s]), axis=0, keepdims=True)
    rows = width // 3
    for i in range(3):
        at = slice(i * rows, (i + 1) * rows)
        total = dot(gproj_ref[0], w_v[0, :, at])
        total += dot(gproj_ref[1], w_v[1, :, at])
        total += dot(gproj_ref[2], w_v[2, :, at])
        part_ref[:, at] = bf16(total)


def fourth_kernel(*refs):
    own_refs, recv_refs, gmid_refs = refs[0:2], refs[2:4], refs[4:6]
    lat_ref, vec_ref, out_ref, stat_ref = refs[6:10]
    tokens, width = own_refs[0].shape
    per_frame = lat_ref.shape[2] // CHUNKS
    step = 2 * per_frame
    stat_ref[...] = jnp.zeros_like(stat_ref)
    for chunk in range(CHUNKS):
        patches = slice(chunk * per_frame, (chunk + 1) * per_frame)

        def leave(row, chunk=chunk, patches=patches):
            at = pl.ds(row, step)
            frames = pl.ds(row // per_frame, 2)
            values = f32(lat_ref[0, frames, patches, :]).reshape(step, width)
            normed, inverse = normalize(values)
            grad_entry = f32(own_refs[chunk][at, :]) + f32(recv_refs[chunk][at, :])
            stat_ref[0:1, :] += jnp.sum(grad_entry, axis=0, keepdims=True)
            stat_ref[1:2, :] += jnp.sum(grad_entry * normed, axis=0, keepdims=True)
            result = gmid_refs[chunk][at, :] + norm_back(
                grad_entry * vec_ref[1:2, :], normed, inverse
            )
            out_ref[0, frames, patches, :] = result.reshape(2, per_frame, width)

        over_rows(tokens, step, leave)


def output_kernel(*refs):
    own_refs, recv_refs, own2_refs, recv2_refs = refs[0:2], refs[2:4], refs[4:6], refs[6:8]
    lat_ref, dy_ref, vec_ref, out_ref, stat_ref = refs[8:13]
    tokens, width = own_refs[0].shape
    per_frame = lat_ref.shape[2] // CHUNKS
    step = 2 * per_frame
    stat_ref[...] = jnp.zeros_like(stat_ref)
    for chunk in range(CHUNKS):
        patches = slice(chunk * per_frame, (chunk + 1) * per_frame)

        def leave(row, chunk=chunk, patches=patches):
            at = pl.ds(row, step)
            frames = pl.ds(row // per_frame, 2)
            values = f32(lat_ref[0, frames, patches, :]).reshape(step, width)
            grad = f32(dy_ref[0, frames, patches, :]).reshape(step, width)
            attention = f32(own_refs[chunk][at, :]) + f32(recv_refs[chunk][at, :]) + vec_ref[6:7, :]
            branch = f32(own2_refs[chunk][at, :]) + f32(recv2_refs[chunk][at, :]) + vec_ref[7:8, :]
            stat_ref[0:1, :] += jnp.sum(grad * branch, axis=0, keepdims=True)
            result = values + vec_ref[2:3, :] * attention + vec_ref[5:6, :] * branch
            out_ref[0, frames, patches, :] = result.reshape(2, per_frame, width)

        over_rows(tokens, step, leave)


def act_grad_kernel(dy_ref, vec_ref, w2_ref, low0_ref, low1_ref, ga0_ref, ga1_ref, sum_ref):
    tokens, width = low0_ref.shape
    per_frame = tokens // dy_ref.shape[1]

    @pl.when(pl.program_id(0) == 0)
    def _():
        sum_ref[...] = jnp.zeros_like(sum_ref)
        for chunk, low_ref in enumerate((low0_ref, low1_ref)):
            step = 2 * per_frame
            patches = slice(chunk * per_frame, (chunk + 1) * per_frame)

            def enter(row, low_ref=low_ref, patches=patches):
                frames = pl.ds(row // per_frame, 2)
                grad = f32(dy_ref[0, frames, patches, :]).reshape(step, width)
                sum_ref[0:1, :] += jnp.sum(grad, axis=0, keepdims=True)
                low_ref[pl.ds(row, step), :] = bf16(grad * vec_ref[5:6, :])

            over_rows(tokens, step, enter)

    ga0_ref[...] = bf16(dot(low0_ref[...], w2_ref[...], NT))
    ga1_ref[...] = bf16(dot(low1_ref[...], w2_ref[...], NT))


def branch_kernel(act_ref, w2_ref, part_ref, sum_v):
    @pl.when(pl.program_id(0) == 0)
    def _():
        sum_v[...] = jnp.zeros_like(sum_v)

    sum_v[...] += dot(act_ref[...], w2_ref[...])

    @pl.when(pl.program_id(0) == pl.num_programs(0) - 1)
    def _():
        part_ref[...] = bf16(sum_v[...])


def weight_grad_kernel(core_ref, a0_ref, a1_ref, b0_ref, b1_ref, keep_ref, send_ref, left_v, tile_v):
    pairs = keep_ref.shape[-3]
    tokens, width = a0_ref.shape
    rows = width // (2 * pairs)
    core = core_ref[0]

    @pl.when(pl.program_id(0) == 0)
    def _():
        left_v[:, :tokens] = a0_ref[...].T
        left_v[:, tokens:] = a1_ref[...].T

    columns = keep_ref.shape[-1]
    right = jnp.concatenate(
        [b0_ref[...].reshape(tokens, columns), b1_ref[...].reshape(tokens, columns)], axis=0
    )
    half = width // 2
    for i in range(2):
        found = dot(left_v[i * half : (i + 1) * half, :], right)
        tile_v[i * pairs : (i + 1) * pairs] = found.reshape(pairs, rows, columns)
    for k in range(pairs):
        keep_ref[k] = bf16(tile_v[2 * k + core])
        send_ref[k] = bf16(tile_v[2 * k + 1 - core])


def weight_grad(core, left, right, dp, tile):
    tokens, width = left[0].shape
    rows = width // dp
    stacked = right[0].ndim == 3
    sections = right[0].shape[0] if stacked else 1
    columns = right[0].shape[-1]
    pairs = dp // 2
    if stacked:
        grid = (sections,)
        tile = columns
        right_spec = pl.BlockSpec((None, tokens, columns), lambda j: (j, 0, 0))
        out_spec = pl.BlockSpec((None, pairs, rows, columns), lambda j: (j, 0, 0, 0))
        shape = (sections, pairs, rows, columns)
    else:
        grid = (columns // tile,)
        right_spec = pl.BlockSpec((tokens, tile), lambda j: (0, j))
        out_spec = pl.BlockSpec((pairs, rows, tile), lambda j: (0, 0, j))
        shape = (pairs, rows, columns)
    left_spec = pl.BlockSpec((tokens, width), lambda j: (0, 0))
    out = jax.ShapeDtypeStruct(shape, jnp.bfloat16)
    return pl.pallas_call(
        weight_grad_kernel,
        grid=grid,
        in_specs=[SMEM, left_spec, left_spec, right_spec, right_spec],
        out_specs=[out_spec, out_spec],
        out_shape=[out, out],
        scratch_shapes=[
            pltpu.VMEM((width, 2 * tokens), jnp.bfloat16),
            pltpu.VMEM((dp, rows, tile), jnp.float32),
        ],
        compiler_params=params(40),
        cost_estimate=cost(
            4 * tokens * width * columns * sections,
            4 * tokens * (width + columns * sections) + 2 * width * columns * sections,
        ),
    )(core, *left, *right)


def pair_swap(values, axis, bit, size):
    return lax.ppermute(values, axis, [(i, i ^ bit) for i in range(size)])


def reduce_to_owner(keep, send, dp, order, lead):
    bits = dp.bit_length() - 1
    shape = keep.shape
    split = shape[:lead] + (2,) * (bits - 1) + shape[lead + 1 :]
    place = lax.axis_index("dp")
    recv = pair_swap(send, "dp", 1, dp)
    keep, recv = keep.reshape(split), recv.reshape(split)
    left = [b for b in range(bits - 1, 0, -1)]
    for count, bit in enumerate(order):
        axis = lead + left.index(bit)
        mine = (place >> bit) & 1

        def half(values, which, axis=axis):
            return lax.dynamic_index_in_dim(values, which, axis, keepdims=False)

        send = bf16(f32(half(keep, 1 - mine)) + f32(half(recv, 1 - mine)))
        arrived = pair_swap(send, "dp", 1 << bit, dp)
        keep = f32(half(keep, mine)) + f32(half(recv, mine))
        if count < len(order) - 1:
            keep = bf16(keep)
        recv = arrived
        left.remove(bit)
    return f32(keep) + f32(recv)


def fits(mesh):
    dp, mp = mesh.shape["dp"], mesh.shape["mp"]
    return mp == 2 and dp == 16


def fast_body(
    latents,
    conditioning,
    clip_mask,
    qkv_weight,
    qv_bias,
    proj_weight,
    proj_bias,
    fc1_weight,
    fc1_bias,
    fc2_weight,
    fc2_bias,
    ada_weight,
    ada_bias,
    out_cotangent,
):
    frames, patches, width = latents.shape[1:]
    local = qkv_weight.shape[2]
    ff = fc1_weight.shape[1]
    dp = lax.axis_size("dp")
    per_frame = patches // CHUNKS
    tokens = frames * per_frame
    row = lax.axis_index("mp")
    place = lax.axis_index("dp")
    core = (place % 2).astype(jnp.int32).reshape(1)

    scaled = jax.nn.silu(conditioning)
    scaled_low = bf16(scaled)
    mod_local = dot(scaled_low, ada_weight) + f32(ada_bias)
    mod_other = pair_swap(mod_local, "mp", 1, 2)
    modulation = jnp.where(
        row == 0,
        jnp.concatenate([mod_local, mod_other], axis=1),
        jnp.concatenate([mod_other, mod_local], axis=1),
    ).reshape(6, width)
    mask_value = f32(clip_mask[0])
    vec = jnp.stack(
        [
            modulation[0],
            1.0 + modulation[1],
            mask_value * modulation[2],
            modulation[3],
            1.0 + modulation[4],
            modulation[5],
            f32(proj_bias),
            f32(fc2_bias),
        ]
    )
    gate_one, gate_two = vec[2], vec[5]
    qkv_rows = jnp.transpose(qkv_weight, (1, 2, 0))
    bias_rows = jnp.stack([f32(qv_bias[0]), jnp.zeros((local,), jnp.float32), f32(qv_bias[1])])
    hidden_bias = f32(fc1_bias)[None, :]

    def chunk_block(c):
        return pl.BlockSpec((1, frames, per_frame, width), lambda i: (0, 0, c, 0))

    def whole(*shape):
        return pl.BlockSpec(shape, lambda i: (0,) * len(shape))

    def struct(*shape, dtype=jnp.bfloat16):
        return jax.ShapeDtypeStruct(shape, dtype)

    def first(c):
        outs = [
            struct(tokens, width),
            struct(3, tokens, local),
            struct(tokens, local),
            struct(tokens, width),
        ]
        return pl.pallas_call(
            first_kernel,
            grid=(1,),
            in_specs=[chunk_block(c), whole(8, width), whole(3, local), ANY, ANY],
            out_specs=[whole(*o.shape) for o in outs],
            out_shape=outs,
            scratch_shapes=[
                pltpu.VMEM((3, local, width), jnp.bfloat16),
                pltpu.VMEM((local, width), jnp.bfloat16),
                pltpu.SemaphoreType.DMA((4,)),
            ],
            compiler_params=params(40),
            cost_estimate=cost(10 * tokens * local * width, 5e6),
        )(latents, vec, bias_rows, qkv_rows, proj_weight)

    firsts = [first(c) for c in range(CHUNKS)]
    part1 = [o[0] for o in firsts]
    projected = [o[1] for o in firsts]
    mixed = [o[2] for o in firsts]
    entry_one = [o[3] for o in firsts]
    recv1 = [pair_swap(p, "mp", 1, 2) for p in part1]

    tile = 256
    token_block = pl.BlockSpec((tokens, width), lambda j: (0, 0))
    low_block = pl.BlockSpec((tokens, tile), lambda j: (0, j))
    branch_low0, branch_low1, ga0, ga1, dy_sum = pl.pallas_call(
        act_grad_kernel,
        grid=(ff // tile,),
        in_specs=[
            pl.BlockSpec((1, frames, patches, width), lambda j: (0, 0, 0, 0)),
            whole(8, width),
            pl.BlockSpec((tile, width), lambda j: (j, 0)),
        ],
        out_specs=[token_block, token_block, low_block, low_block, whole(8, width)],
        out_shape=[
            struct(tokens, width),
            struct(tokens, width),
            struct(tokens, ff),
            struct(tokens, ff),
            struct(8, width, dtype=jnp.float32),
        ],
        compiler_params=params(40),
        cost_estimate=cost(4 * tokens * width * ff, 1e7),
    )(out_cotangent, vec, fc2_weight)
    branch_low = [branch_low0, branch_low1]
    act_grad = [ga0, ga1]

    def second(c):
        outs = [
            struct(tokens, width),
            struct(tokens, width),
            struct(tokens, ff),
            struct(tokens, ff),
            struct(1, ff, dtype=jnp.float32),
        ]
        return pl.pallas_call(
            second_kernel,
            grid=(1,),
            in_specs=[
                whole(tokens, width),
                whole(tokens, width),
                chunk_block(c),
                whole(8, width),
                whole(1, ff),
                whole(tokens, ff),
                ANY,
            ],
            out_specs=[whole(*o.shape) for o in outs],
            out_shape=outs,
            scratch_shapes=[
                pltpu.VMEM((width, ff), jnp.bfloat16),
                pltpu.SemaphoreType.DMA((3,)),
            ],
            compiler_params=params(40),
            cost_estimate=cost(4 * tokens * ff * width, 1e7),
        )(part1[c], recv1[c], latents, vec, hidden_bias, act_grad[c], fc1_weight)

    seconds = [second(c) for c in range(CHUNKS)]
    part3 = [o[0] for o in seconds]
    entry_two = [o[1] for o in seconds]
    activated = [o[2] for o in seconds]
    hidden_low = [o[3] for o in seconds]
    hidden_sum = sum(o[4] for o in seconds)
    recv3 = [pair_swap(p, "mp", 1, 2) for p in part3]

    def branch_part(c):
        deep = 384
        return pl.pallas_call(
            branch_kernel,
            grid=(ff // deep,),
            in_specs=[
                pl.BlockSpec((tokens, deep), lambda k: (0, k)),
                pl.BlockSpec((deep, width), lambda k: (k, 0)),
            ],
            out_specs=token_block,
            out_shape=struct(tokens, width),
            scratch_shapes=[pltpu.VMEM((tokens, width), jnp.float32)],
            compiler_params=params(24),
            cost_estimate=cost(2 * tokens * ff * width, 7e6),
        )(activated[c], fc2_weight)

    part2 = [branch_part(c) for c in range(CHUNKS)]
    recv2 = [pair_swap(p, "mp", 1, 2) for p in part2]

    keep2, send2 = weight_grad(core, branch_low, activated, dp, tile)
    keep1, send1 = weight_grad(core, entry_two, hidden_low, dp, tile)

    def third(c):
        outs = [
            struct(tokens, width),
            struct(3, tokens, local),
            struct(tokens, width),
            struct(tokens, width, dtype=jnp.float32),
            struct(8, width, dtype=jnp.float32),
            struct(3, local, dtype=jnp.float32),
        ]
        return pl.pallas_call(
            third_kernel,
            grid=(1,),
            in_specs=[whole(tokens, width)] * 4
            + [chunk_block(c), chunk_block(c), whole(8, width), whole(3, tokens, local), ANY, ANY],
            out_specs=[whole(*o.shape) for o in outs],
            out_shape=outs,
            scratch_shapes=[
                pltpu.VMEM((3, local, width), jnp.bfloat16),
                pltpu.VMEM((local, width), jnp.bfloat16),
                pltpu.VMEM((tokens, local), jnp.bfloat16),
                pltpu.SemaphoreType.DMA((4,)),
            ],
            compiler_params=params(40),
            cost_estimate=cost(14 * tokens * local * width, 1e7),
        )(
            part1[c],
            recv1[c],
            part3[c],
            recv3[c],
            latents,
            out_cotangent,
            vec,
            projected[c],
            qkv_rows,
            proj_weight,
        )

    thirds = [third(c) for c in range(CHUNKS)]
    part4 = [o[0] for o in thirds]
    grad_projected = [o[1] for o in thirds]
    attention_low = [o[2] for o in thirds]
    grad_middle = [o[3] for o in thirds]
    stats = sum(o[4] for o in thirds)
    qkv_sums = sum(o[5] for o in thirds)
    recv4 = [pair_swap(p, "mp", 1, 2) for p in part4]

    keep_q, send_q = weight_grad(core, entry_one, grad_projected, dp, local)
    keep_p, send_p = weight_grad(core, attention_low, mixed, dp, local)

    full = pl.BlockSpec((1, frames, patches, width), lambda i: (0, 0, 0, 0))
    out_shapes = [
        struct(*latents.shape, dtype=jnp.float32),
        struct(8, width, dtype=jnp.float32),
    ]
    output, out_stats = pl.pallas_call(
        output_kernel,
        grid=(1,),
        in_specs=[whole(tokens, width)] * 8 + [full, full, whole(8, width)],
        out_specs=[full, whole(8, width)],
        out_shape=out_shapes,
        compiler_params=params(40),
        cost_estimate=cost(1e7, 1e7),
    )(*part1, *recv1, *part2, *recv2, latents, out_cotangent, vec)
    grad_latents, last_stats = pl.pallas_call(
        fourth_kernel,
        grid=(1,),
        in_specs=[whole(tokens, width)] * 6 + [full, whole(8, width)],
        out_specs=[full, whole(8, width)],
        out_shape=out_shapes,
        compiler_params=params(40),
        cost_estimate=cost(1e7, 1e7),
    )(*part4, *recv4, *grad_middle, latents, vec)

    fc2_total = reduce_to_owner(keep2, send2, dp, (1, 2, 3), 0)
    fc1_total = reduce_to_owner(keep1, send1, dp, (2, 1, 3), 0)
    qkv_total = reduce_to_owner(keep_q, send_q, dp, (1, 2, 3), 1)
    proj_total = reduce_to_owner(keep_p, send_p, dp, (2, 1, 3), 0)

    grad_modulation = jnp.concatenate(
        [
            last_stats[0],
            last_stats[1],
            mask_value * stats[2],
            stats[0],
            stats[1],
            out_stats[0],
        ]
    )
    local_cols = ada_weight.shape[1]
    grad_mod_local = lax.dynamic_slice_in_dim(grad_modulation, row * local_cols, local_cols)
    modulation_low = bf16(grad_mod_local)[None, :]
    scaled_part = dot(modulation_low, ada_weight, NT)
    grad_scaled = scaled_part + pair_swap(scaled_part, "mp", 1, 2)
    grad_cond = jax.vjp(jax.nn.silu, conditioning)[1](grad_scaled)[0]

    pieces = [
        grad_mod_local,
        f32(scaled_low[0]),
        qkv_sums[0],
        qkv_sums[2],
        gate_one * stats[3],
        hidden_sum[0],
        gate_two * dy_sum[0],
    ]
    gathered = lax.all_gather(jnp.concatenate(pieces), "dp", axis=0)
    ends = [0]
    for piece in pieces:
        ends.append(ends[-1] + piece.shape[0])
    items_mod = gathered[:, : ends[1]]
    items_scaled = gathered[:, ends[1] : ends[2]]
    sums = jnp.sum(gathered, axis=0)
    block = width // dp
    mine = lax.dynamic_slice_in_dim(items_scaled, place * block, block, axis=1)
    grad_ada = dot(bf16(mine), bf16(items_mod), TN)
    qv_total = sums[ends[2] : ends[4]].reshape(2, local)
    return (
        output,
        grad_latents,
        grad_cond,
        jnp.transpose(qkv_total, (1, 0, 2)),
        qv_total,
        proj_total.T,
        sums[ends[4] : ends[5]],
        fc1_total,
        sums[ends[5] : ends[6]],
        fc2_total.T,
        sums[ends[6] : ends[7]],
        grad_ada,
        sums[: ends[1]],
    )


def solution(mesh):
    body = fast_body if fits(mesh) else general_body
    return jax.shard_map(
        body,
        mesh=mesh,
        in_specs=(
            P("dp", None, None, None),
            P("dp", None),
            P("dp"),
            P(None, None, "mp"),
            P(None, "mp"),
            P("mp", None),
            P(),
            P(None, "mp"),
            P("mp"),
            P("mp", None),
            P(),
            P(None, "mp"),
            P("mp"),
            P("dp", None, None, None),
        ),
        out_specs=(
            P("dp", None, None, None),
            P("dp", None, None, None),
            P("dp", None),
            P("dp", None, "mp"),
            P(None, "mp"),
            P("mp", "dp"),
            P(),
            P("dp", "mp"),
            P("mp"),
            P("mp", "dp"),
            P(),
            P("dp", "mp"),
            P("mp"),
        ),
        check_vma=False,
    )
```

```python
from functools import partial

import jax
import jax.numpy as jnp
from jax import lax
from jax.experimental import pallas as pl
from jax.experimental.pallas import tpu as pltpu
from jax.sharding import PartitionSpec as P

HEAD_DIM = 72


def normalize(values):
    centered = values - jnp.mean(values, axis=-1, keepdims=True)
    inverse = lax.rsqrt(jnp.mean(centered * centered, axis=-1, keepdims=True) + 1e-06)
    return (centered * inverse, inverse)


def norm_back(grad_normed, normed, inverse):
    first = jnp.mean(grad_normed, axis=-1, keepdims=True)
    second = jnp.mean(grad_normed * normed, axis=-1, keepdims=True)
    return inverse * (grad_normed - first - normed * second)


def general_body(
    latents,
    conditioning,
    clip_mask,
    qkv_weight,
    qv_bias,
    proj_weight,
    proj_bias,
    fc1_weight,
    fc1_bias,
    fc2_weight,
    fc2_bias,
    ada_weight,
    ada_bias,
    out_cotangent,
):
    frames = latents.shape[1]
    patches = latents.shape[2]
    width = latents.shape[3]
    tok_count = frames * patches
    local_width = qkv_weight.shape[2]
    local_heads = local_width // HEAD_DIM
    factor = HEAD_DIM ** (-0.5)
    stream = latents.reshape(tok_count, width).astype(jnp.float32)
    scaled = jax.nn.silu(conditioning)
    scaled_low = scaled.astype(jnp.bfloat16)
    mod_local = jnp.dot(
        scaled_low, ada_weight, preferred_element_type=jnp.float32
    ) + ada_bias.astype(jnp.float32)
    modulation = lax.all_gather(mod_local, "mp", axis=1, tiled=True).reshape(6, width)
    shift_one = modulation[0]
    scale_one = modulation[1]
    gate_one = modulation[2]
    shift_two = modulation[3]
    scale_two = modulation[4]
    gate_two = modulation[5]
    is_clip = clip_mask[0] > 0
    mask_value = clip_mask[0].astype(jnp.float32)
    normed_one, inverse_one = normalize(stream)
    entry_one = (normed_one * (1.0 + scale_one) + shift_one).astype(jnp.bfloat16)
    qkv_flat = qkv_weight.reshape(width, 3 * local_width)
    bias_rows = qv_bias.astype(jnp.float32)
    bias_full = jnp.stack([bias_rows[0], jnp.zeros_like(bias_rows[0]), bias_rows[1]]).reshape(
        3 * local_width
    )

    def split_heads(projected):
        parts = projected.reshape(frames, patches, 3, local_heads, HEAD_DIM)
        return (parts[:, :, 0], parts[:, :, 1], parts[:, :, 2])

    def softmax_weights(query, keys):
        scores = (
            jnp.einsum("fphd,gphd->phfg", query, keys, preferred_element_type=jnp.float32) * factor
        )
        return jax.nn.softmax(scores, axis=-1)

    def attn_forward(entry):
        projected = (
            jnp.dot(entry, qkv_flat, preferred_element_type=jnp.float32) + bias_full
        ).astype(jnp.bfloat16)
        query, keys, values = split_heads(projected)
        weights = softmax_weights(query, keys)
        mixed = jnp.einsum(
            "phfg,gphd->fphd",
            weights.astype(jnp.bfloat16),
            values,
            preferred_element_type=jnp.float32,
        )
        mixed = mixed.astype(jnp.bfloat16).reshape(tok_count, local_width)
        partial_out = jnp.dot(mixed, proj_weight, preferred_element_type=jnp.float32)
        return (partial_out, projected, mixed)

    def attn_skip(entry):
        return (
            jnp.zeros((tok_count, width), jnp.float32),
            jnp.zeros((tok_count, 3 * local_width), jnp.bfloat16),
            jnp.zeros((tok_count, local_width), jnp.bfloat16),
        )

    partial_out, projected, mixed = lax.cond(is_clip, attn_forward, attn_skip, entry_one)
    attention = lax.psum(partial_out.astype(jnp.bfloat16), "mp").astype(
        jnp.float32
    ) + proj_bias.astype(jnp.float32)
    middle = stream + mask_value * gate_one * attention
    normed_two, inverse_two = normalize(middle)
    entry_two = (normed_two * (1.0 + scale_two) + shift_two).astype(jnp.bfloat16)
    hidden = jnp.dot(entry_two, fc1_weight, preferred_element_type=jnp.float32) + fc1_bias.astype(
        jnp.float32
    )
    activated = jax.nn.gelu(hidden, approximate=True).astype(jnp.bfloat16)
    branch_part = jnp.dot(activated, fc2_weight, preferred_element_type=jnp.float32)
    branch = lax.psum(branch_part.astype(jnp.bfloat16), "mp").astype(jnp.float32) + fc2_bias.astype(
        jnp.float32
    )
    output = middle + gate_two * branch
    grad_out = out_cotangent.reshape(tok_count, width).astype(jnp.float32)
    grad_branch = gate_two * grad_out
    grad_fc2_bias = jnp.sum(grad_branch, axis=0)
    branch_low = grad_branch.astype(jnp.bfloat16)
    grad_fc2 = jnp.einsum("ti,tj->ij", activated, branch_low, preferred_element_type=jnp.float32)
    grad_act = jnp.einsum("tj,ij->ti", branch_low, fc2_weight, preferred_element_type=jnp.float32)
    grad_hidden = jax.vjp(partial(jax.nn.gelu, approximate=True), hidden)[1](grad_act)[0]
    grad_fc1_bias = jnp.sum(grad_hidden, axis=0)
    hidden_low = grad_hidden.astype(jnp.bfloat16)
    grad_fc1 = jnp.einsum("ti,tj->ij", entry_two, hidden_low, preferred_element_type=jnp.float32)
    entry_two_part = jnp.einsum(
        "tj,ij->ti", hidden_low, fc1_weight, preferred_element_type=jnp.float32
    )
    grad_entry_two = lax.psum(entry_two_part.astype(jnp.bfloat16), "mp").astype(jnp.float32)
    grad_gate_two = jnp.sum(grad_out * branch, axis=0)
    grad_shift_two = jnp.sum(grad_entry_two, axis=0)
    grad_scale_two = jnp.sum(grad_entry_two * normed_two, axis=0)
    grad_middle = grad_out + norm_back(grad_entry_two * (1.0 + scale_two), normed_two, inverse_two)
    grad_gate_one = mask_value * jnp.sum(grad_middle * attention, axis=0)
    grad_attention = mask_value * gate_one * grad_middle
    grad_proj_bias = jnp.sum(grad_attention, axis=0)
    attention_low = grad_attention.astype(jnp.bfloat16)

    def attn_backward(operands):
        grad_low, kept_projected, kept_mixed = operands
        grad_proj = jnp.einsum(
            "ti,tj->ij", kept_mixed, grad_low, preferred_element_type=jnp.float32
        )
        grad_mixed = jnp.einsum(
            "tj,ij->ti", grad_low, proj_weight, preferred_element_type=jnp.float32
        )
        grad_mixed = grad_mixed.astype(jnp.bfloat16).reshape(frames, patches, local_heads, HEAD_DIM)
        query, keys, values = split_heads(kept_projected)
        weights = softmax_weights(query, keys)
        grad_values = jnp.einsum(
            "phfg,fphd->gphd",
            weights.astype(jnp.bfloat16),
            grad_mixed,
            preferred_element_type=jnp.float32,
        )
        grad_weights = jnp.einsum(
            "fphd,gphd->phfg", grad_mixed, values, preferred_element_type=jnp.float32
        )
        grad_scores = weights * (
            grad_weights - jnp.sum(weights * grad_weights, axis=-1, keepdims=True)
        )
        grad_scores = grad_scores.astype(jnp.bfloat16)
        grad_query = (
            jnp.einsum("phfg,gphd->fphd", grad_scores, keys, preferred_element_type=jnp.float32)
            * factor
        )
        grad_keys = (
            jnp.einsum("phfg,fphd->gphd", grad_scores, query, preferred_element_type=jnp.float32)
            * factor
        )
        grad_all = (
            jnp.stack([grad_query, grad_keys, grad_values], axis=2)
            .astype(jnp.bfloat16)
            .reshape(tok_count, 3 * local_width)
        )
        column_sums = jnp.sum(grad_all.astype(jnp.float32), axis=0).reshape(3, local_width)
        grad_qv = jnp.stack([column_sums[0], column_sums[2]])
        grad_qkv = jnp.einsum(
            "ti,tj->ij", entry_one, grad_all, preferred_element_type=jnp.float32
        ).reshape(width, 3, local_width)
        grad_entry = jnp.einsum("tj,ij->ti", grad_all, qkv_flat, preferred_element_type=jnp.float32)
        return (grad_proj, grad_qv, grad_qkv, grad_entry)

    def skip_backward(operands):
        return (
            jnp.zeros((local_width, width), jnp.float32),
            jnp.zeros((2, local_width), jnp.float32),
            jnp.zeros((width, 3, local_width), jnp.float32),
            jnp.zeros((tok_count, width), jnp.float32),
        )

    grad_proj, grad_qv, grad_qkv, entry_one_part = lax.cond(
        is_clip, attn_backward, skip_backward, (attention_low, projected, mixed)
    )
    grad_entry_one = lax.psum(entry_one_part.astype(jnp.bfloat16), "mp").astype(jnp.float32)
    grad_shift_one = jnp.sum(grad_entry_one, axis=0)
    grad_scale_one = jnp.sum(grad_entry_one * normed_one, axis=0)
    grad_latents = grad_middle + norm_back(
        grad_entry_one * (1.0 + scale_one), normed_one, inverse_one
    )
    grad_modulation = jnp.concatenate(
        [
            grad_shift_one,
            grad_scale_one,
            grad_gate_one,
            grad_shift_two,
            grad_scale_two,
            grad_gate_two,
        ]
    )
    local_cols = ada_weight.shape[1]
    grad_mod_local = lax.dynamic_slice_in_dim(
        grad_modulation, lax.axis_index("mp") * local_cols, local_cols
    )[None, :]
    grad_ada_bias = jnp.sum(grad_mod_local, axis=0)
    modulation_low = grad_mod_local.astype(jnp.bfloat16)
    scaled_part = jnp.einsum(
        "tj,ij->ti", modulation_low, ada_weight, preferred_element_type=jnp.float32
    )
    grad_scaled = lax.psum(scaled_part, "mp")
    grad_cond = jax.vjp(jax.nn.silu, conditioning)[1](grad_scaled)[0]
    ada_term = jnp.einsum(
        "ti,tj->ij", scaled_low, modulation_low, preferred_element_type=jnp.float32
    )
    grad_ada = lax.psum_scatter(
        ada_term.astype(jnp.bfloat16), "dp", scatter_dimension=0, tiled=True
    ).astype(jnp.float32)
    qkv_total, proj_total, fc1_total, fc2_total = (
        lax.psum_scatter(
            grad_qkv.astype(jnp.bfloat16), "dp", scatter_dimension=0, tiled=True
        ).astype(jnp.float32),
        lax.psum_scatter(
            grad_proj.astype(jnp.bfloat16), "dp", scatter_dimension=1, tiled=True
        ).astype(jnp.float32),
        lax.psum_scatter(
            grad_fc1.astype(jnp.bfloat16), "dp", scatter_dimension=0, tiled=True
        ).astype(jnp.float32),
        lax.psum_scatter(
            grad_fc2.astype(jnp.bfloat16), "dp", scatter_dimension=1, tiled=True
        ).astype(jnp.float32),
    )
    qv_total, proj_bias_total, fc1_bias_total, fc2_bias_total, ada_bias_total = lax.psum(
        (grad_qv, grad_proj_bias, grad_fc1_bias, grad_fc2_bias, grad_ada_bias), "dp"
    )
    return (
        output.reshape(latents.shape),
        grad_latents.reshape(latents.shape),
        grad_cond,
        qkv_total,
        qv_total,
        proj_total,
        proj_bias_total,
        fc1_total,
        fc1_bias_total,
        fc2_total,
        fc2_bias_total,
        grad_ada,
        ada_bias_total,
    )


NT = (((1,), (1,)), ((), ()))
TN = (((0,), (0,)), ((), ()))
CHUNKS = 2
TILE = 256
GELU_A = 0.7978845608028654
GELU_B = 0.044715
VMEM = pl.BlockSpec(memory_space=pltpu.VMEM)
ANY = pl.BlockSpec(memory_space=pl.ANY)
ORDERS = ((1, 2, 3), (1, 2, 3), (2, 1, 3), (1, 2, 3), (1, 2, 3), (1, 2, 3), (1, 2, 3), (1, 2, 3), (2, 1, 3), (1, 2, 3))


def f32(values):
    return values.astype(jnp.float32)


def bf16(values):
    return values.astype(jnp.bfloat16)


def dot(left, right, dims=(((1,), (0,)), ((), ()))):
    return lax.dot_general(left, right, dims, preferred_element_type=jnp.float32)


def repeat(count, visit):
    def at(i, carry):
        visit(i)
        return carry

    lax.fori_loop(0, count, at, 0)


def head_spans(width):
    spans = []
    for head in range(width // HEAD_DIM):
        first, last = head * HEAD_DIM, (head + 1) * HEAD_DIM
        low = first // 128 * 128
        high = min(-(-last // 128) * 128, width)
        spans.append((first, last, low, high))
    return spans


def lane_mask(first, last, low, high):
    lane = lax.broadcasted_iota(jnp.int32, (1, high - low), 1) + low
    return (lane >= first) & (lane < last)


def same_patch(tokens, per_frame):
    row = lax.broadcasted_iota(jnp.int32, (tokens, tokens), 0)
    col = lax.broadcasted_iota(jnp.int32, (tokens, tokens), 1)
    return (row % per_frame) == (col % per_frame)


def attention_weights(query, keys, allowed):
    scores = dot(query, keys, NT) * (HEAD_DIM ** (-0.5))
    scores = jnp.where(allowed, scores, -1e30)
    grown = jnp.exp(scores - jnp.max(scores, axis=-1, keepdims=True))
    return grown / jnp.sum(grown, axis=-1, keepdims=True)


def column_blocks(width, block):
    return [(low, min(block, width - low)) for low in range(0, width, block)]


def block_kernel(
    lat_ref,
    dy_ref,
    vec_ref,
    bias_ref,
    b1_ref,
    w_hbm,
    pw_hbm,
    w1_hbm,
    w2_hbm,
    out_hbm,
    glat_hbm,
    rs2_ref,
    rs1_ref,
    rsq_ref,
    stat_ref,
    hsum_ref,
    qsum_ref,
    wide_v,
    w2_v,
    e1_v,
    proj_v,
    mixed_v,
    e2_v,
    act_v,
    low_v,
    bl_v,
    part1_v,
    recv1_v,
    part2_v,
    recv2_v,
    part3_v,
    recv3_v,
    recv4_v,
    gmid_v,
    stage_v,
    left_v,
    tile_v,
    keep_a,
    keep_b,
    later_a,
    later_b,
    send0_v,
    recv0_v,
    load_sem,
    y_send,
    y_recv,
    rs_send,
    rs_recv,
    credit,
):
    frames, patches, width = lat_ref.shape[1:]
    per_frame = patches // CHUNKS
    tokens = frames * per_frame
    local = proj_v.shape[3]
    padded = mixed_v.shape[2]
    ff = act_v.shape[2]
    planes, rows = send0_v.shape[1], send0_v.shape[2]
    place = lax.axis_index("dp")
    across = 1 - lax.axis_index("mp")
    bit_of = [(place // (1 << b)) % 2 for b in range(4)]
    partner = [place + (1 - 2 * bit_of[b]) * (1 << b) for b in range(4)]
    core = bit_of[0]

    barrier = pltpu.get_barrier_semaphore()
    pl.semaphore_signal(barrier, inc=1, device_id={"mp": across}, device_id_type=pl.DeviceIdType.MESH)
    for other in partner:
        pl.semaphore_signal(barrier, inc=1, device_id={"dp": other}, device_id_type=pl.DeviceIdType.MESH)

    def load(source, target, index):
        copy = pltpu.make_async_copy(source, target, load_sem.at[index])
        copy.start()
        return copy

    def load_attention(index):
        copies = [
            load(w_hbm.at[s], wide_v.at[s * local : (s + 1) * local, :], index + s) for s in range(3)
        ]
        return copies + [load(pw_hbm, wide_v.at[3 * local :, :], index + 3)]

    def load_hidden(index):
        return [
            load(w1_hbm.at[:, i * width : (i + 1) * width], wide_v.at[i * width : (i + 1) * width, :], index + i)
            for i in range(2)
        ]

    attention_loads = load_attention(0)
    w2_load = load(w2_hbm, w2_v, 4)
    stat_ref[...] = jnp.zeros_like(stat_ref)

    step = 2 * per_frame

    def token_rows(ref, chunk, i):
        block = ref[0, pl.ds(2 * i, 2), chunk * per_frame : (chunk + 1) * per_frame, :]
        return f32(block).reshape(step, width)

    def over_rows(visit):
        repeat(tokens // step, lambda i: visit(i, pl.ds(pl.multiple_of(i * step, step), step)))

    def swap(source, target, index):
        copy = pltpu.make_async_remote_copy(
            src_ref=source,
            dst_ref=target,
            send_sem=y_send.at[index],
            recv_sem=y_recv.at[index],
            device_id={"mp": across},
            device_id_type=pl.DeviceIdType.MESH,
        )
        copy.start()
        return copy

    def add_stat(row, values):
        stat_ref[row : row + 1, :] += jnp.sum(values, axis=0, keepdims=True)

    allowed = same_patch(tokens, per_frame)
    spans = head_spans(local)
    factor = HEAD_DIM ** (-0.5)

    def first_stage(c):
        def enter(i, at):
            normed, _ = normalize(token_rows(lat_ref, c, i))
            e1_v[c, at, :] = bf16(normed * vec_ref[1:2, :] + vec_ref[0:1, :])

        over_rows(enter)
        for s in range(3):
            if c == 0:
                attention_loads[s].wait()
            weight = wide_v[s * local : (s + 1) * local, :]
            proj_v[c, s] = bf16(dot(e1_v[c], weight, NT) + bias_ref[s : s + 1, :])
        mixed_v[c, :, padded - 128 :] = jnp.zeros((tokens, 128), jnp.bfloat16)
        for first, last, low, high in spans:
            mask = lane_mask(first, last, low, high)
            query = jnp.where(mask, proj_v[c, 0, :, low:high], 0)
            weights = attention_weights(query, proj_v[c, 1, :, low:high], allowed)
            mixed = dot(bf16(weights), proj_v[c, 2, :, low:high])
            mixed_v[c, :, low:high] = bf16(jnp.where(mask, mixed, f32(mixed_v[c, :, low:high])))
        if c == 0:
            attention_loads[3].wait()
        part1_v[c] = bf16(dot(mixed_v[c, :, :local], wide_v[3 * local :, :]))

    def act_grad_stage(c):
        def enter(i, at):
            grad = token_rows(dy_ref, c, i)
            add_stat(7, grad)
            bl_v[c, at, :] = bf16(grad * vec_ref[5:6, :])

        over_rows(enter)

        def columns(j):
            at = pl.ds(pl.multiple_of(j * TILE, TILE), TILE)
            low_v[c, :, at] = bf16(dot(bl_v[c], w2_v[at, :], NT))

        repeat(ff // TILE, columns)

    def middle_rows(c, i, at):
        attention = f32(part1_v[c, at, :]) + f32(recv1_v[c, at, :]) + vec_ref[6:7, :]
        return attention, token_rows(lat_ref, c, i) + vec_ref[2:3, :] * attention

    def second_stage(c):
        def enter(i, at):
            _, middle = middle_rows(c, i, at)
            normed, _ = normalize(middle)
            e2_v[c, at, :] = bf16(normed * vec_ref[4:5, :] + vec_ref[3:4, :])

        over_rows(enter)

        def half(i):
            base = pl.multiple_of(i * width, width)
            for low, size in column_blocks(width, TILE):
                at = pl.ds(pl.multiple_of(base + low, 128), size)
                hidden = dot(e2_v[c], wide_v[pl.ds(base, width), low : low + size]) + b1_ref[:, at]
                square = hidden * hidden
                bent = jnp.tanh(GELU_A * hidden * (1.0 + GELU_B * square))
                gate = 0.5 * (1.0 + bent)
                act_v[c, :, at] = bf16(hidden * gate)
                slope = gate + 0.5 * hidden * (1.0 - bent * bent) * (
                    GELU_A * (1.0 + 3.0 * GELU_B * square)
                )
                grad_hidden = f32(low_v[c, :, at]) * slope
                found = jnp.sum(grad_hidden, axis=0, keepdims=True)
                hsum_ref[:, at] = found if c == 0 else hsum_ref[:, at] + found
                low_v[c, :, at] = bf16(grad_hidden)

        repeat(ff // width, half)
        for low, size in column_blocks(width, 2 * TILE):
            total = dot(low_v[c, :, :width], wide_v[low : low + size, :], NT)
            total += dot(low_v[c, :, width:], wide_v[width + low : width + low + size, :], NT)
            part3_v[c, :, low : low + size] = bf16(total)

    def branch_stage(c):
        for low, size in column_blocks(width, 2 * TILE):
            part2_v[c, :, low : low + size] = bf16(dot(act_v[c], w2_v[:, low : low + size]))

    def third_stage(c):
        grads = [act_v.at[c, :, s * padded : (s + 1) * padded] for s in range(3)]
        alow = low_v.at[c, :, :width]
        mixed_grad = low_v.at[c, :, width : width + padded]

        def enter(i, at):
            attention, middle = middle_rows(c, i, at)
            normed, inverse = normalize(middle)
            grad_entry = f32(part3_v[c, at, :]) + f32(recv3_v[c, at, :])
            add_stat(0, grad_entry)
            add_stat(1, grad_entry * normed)
            grad_middle = token_rows(dy_ref, c, i) + norm_back(
                grad_entry * vec_ref[4:5, :], normed, inverse
            )
            add_stat(2, grad_middle * attention)
            add_stat(3, grad_middle)
            gmid_v[c, pl.ds(2 * i, 2)] = grad_middle.reshape(2, per_frame, width)
            alow[at, :] = bf16(vec_ref[2:3, :] * grad_middle)

        over_rows(enter)
        if c == 0:
            reloads[3].wait()
        mixed_grad[:, :local] = bf16(dot(alow[...], wide_v[3 * local :, :], NT))
        for first, last, low, high in spans:
            mask = lane_mask(first, last, low, high)
            query, keys, values = (proj_v[c, s, :, low:high] for s in range(3))
            grad_mixed = mixed_grad[:, low:high]
            weights = attention_weights(jnp.where(mask, query, 0), keys, allowed)
            grad_weights = dot(jnp.where(mask, grad_mixed, 0), values, NT)
            grad_scores = bf16(
                weights * (grad_weights - jnp.sum(weights * grad_weights, axis=-1, keepdims=True))
            )
            found = (
                dot(grad_scores, keys) * factor,
                dot(grad_scores, query, TN) * factor,
                dot(bf16(weights), grad_mixed, TN),
            )
            for s in range(3):
                grads[s][:, low:high] = bf16(jnp.where(mask, found[s], f32(grads[s][:, low:high])))
        for s in range(3):
            if c == 0:
                reloads[s].wait()
            found = jnp.sum(f32(grads[s][:, :local]), axis=0, keepdims=True)
            if c == 0:
                qsum_ref[s : s + 1, :] = found
            else:
                qsum_ref[s : s + 1, :] += found
        swaps3[c].wait_send()
        for low, size in column_blocks(width, 2 * TILE):
            at = slice(low, low + size)
            total = dot(grads[0][:, :local], wide_v[:local, at])
            total += dot(grads[1][:, :local], wide_v[local : 2 * local, at])
            total += dot(grads[2][:, :local], wide_v[2 * local : 3 * local, at])
            part3_v[c, :, at] = bf16(total)

    def last_stage(c):
        def leave(i, at):
            normed, inverse = normalize(token_rows(lat_ref, c, i))
            grad_entry = f32(part3_v[c, at, :]) + f32(recv4_v[c, at, :])
            add_stat(4, grad_entry)
            add_stat(5, grad_entry * normed)
            result = norm_back(grad_entry * vec_ref[1:2, :], normed, inverse)
            gmid_v[c, pl.ds(2 * i, 2)] += result.reshape(2, per_frame, width)

        over_rows(leave)
        return load(
            gmid_v.at[c], glat_hbm.at[0, :, c * per_frame : (c + 1) * per_frame, :], 11 + c
        )

    def output_stage(c):
        def leave(i, at):
            _, middle = middle_rows(c, i, at)
            branch = f32(part2_v[c, at, :]) + f32(recv2_v[c, at, :]) + vec_ref[7:8, :]
            add_stat(6, token_rows(dy_ref, c, i) * branch)
            stage_v[pl.ds(2 * i, 2)] = (middle + vec_ref[5:6, :] * branch).reshape(
                2, per_frame, width
            )

        over_rows(leave)
        return load(stage_v, out_hbm.at[0, :, c * per_frame : (c + 1) * per_frame, :], 13 + c)

    third = send0_v.shape[3]
    started = {}

    def unit_refs(u):
        if u < 6:
            return keep_a.at[u], later_a.at[u], third
        return keep_b.at[u - 6], later_b.at[u - 6], padded

    def left_side(source):
        for c in range(CHUNKS):
            left_v[:, c * tokens : (c + 1) * tokens] = source(c).T

    def weight_unit(u, right):
        keep, _, columns = unit_refs(u)
        slot = u % 3
        if u >= 3:
            started[u - 3, 0].wait_send()
        send = send0_v.at[slot]

        def part(low, size):
            block = jnp.concatenate([right(c, low, size) for c in range(CHUNKS)], axis=0)
            half = width // 2
            for i in range(2):
                found = dot(left_v[i * half : (i + 1) * half, :], block)
                tile_v[i * planes : (i + 1) * planes, :, :size] = found.reshape(planes, rows, size)
            first, second, third_bit = ORDERS[u]
            for j in range(planes):
                even = (j // 4 << first) + (j // 2 % 2 << second) + (j % 2 << third_bit)
                keep[j, :, pl.ds(low, size)] = bf16(tile_v[even + core, :, :size])
                send[j, :, pl.ds(low, size)] = bf16(tile_v[even + 1 - core, :, :size])

        if columns % TILE == 0:
            repeat(columns // TILE, lambda t: part(pl.multiple_of(t * TILE, TILE), TILE))
        else:
            for low, size in column_blocks(columns, TILE):
                part(low, size)
        if u >= 3:
            pl.semaphore_wait(credit.at[slot], 1)
        copy = pltpu.make_async_remote_copy(
            src_ref=send.at[:, :, 0:columns],
            dst_ref=recv0_v.at[slot, :, :, 0:columns],
            send_sem=rs_send.at[u, 0],
            recv_sem=rs_recv.at[u, 0],
            device_id={"dp": partner[0]},
            device_id_type=pl.DeviceIdType.MESH,
        )
        copy.start()
        started[u, 0] = copy

    def advance(u, stage):
        keep, later, columns = unit_refs(u)
        slot = u % 3
        order = ORDERS[u]
        started[u, stage - 1].wait_recv()
        base = sum(bit_of[order[i]] * (4 >> i) for i in range(stage - 1))
        if stage == 1:
            come = recv0_v.at[slot, :, :, 0:columns]
        else:
            come = later.at[(0, 4, 6)[stage - 2] :]
        if stage == 4:
            total = f32(keep[base]) + f32(come[0])
            if u < 3:
                rs2_ref[:, u * third : (u + 1) * third] = total
            elif u < 6:
                rs1_ref[:, (u - 3) * third : (u - 2) * third] = total
            else:
                rsq_ref[u - 6] = total
            return
        count = 4 >> (stage - 1)
        mine = bit_of[order[stage - 1]]

        def add(which):
            def one(i):
                at = which * count + i
                keep[base + at] = bf16(f32(keep[base + at]) + f32(come[at]))

            repeat(count, one)

        add(1 - mine)
        other = partner[order[stage - 1]]
        copy = pltpu.make_async_remote_copy(
            src_ref=keep.at[pl.ds(base + (1 - mine) * count, count)],
            dst_ref=later.at[(0, 4, 6)[stage - 1] : (0, 4, 6)[stage - 1] + count],
            send_sem=rs_send.at[u, stage],
            recv_sem=rs_recv.at[u, stage],
            device_id={"dp": other},
            device_id_type=pl.DeviceIdType.MESH,
        )
        copy.start()
        started[u, stage] = copy
        add(mine)
        if stage == 1 and u < 7:
            pl.semaphore_signal(
                credit.at[slot],
                inc=1,
                device_id={"dp": partner[0]},
                device_id_type=pl.DeviceIdType.MESH,
            )

    def hidden_unit(u, right_v):
        weight_unit(u, lambda c, low, size: right_v[c, :, pl.ds((u % 3) * third + low, size)])

    pl.semaphore_wait(barrier, 5)
    first_stage(0)
    swaps1 = [swap(part1_v.at[0], recv1_v.at[0], 0)]
    first_stage(1)
    swaps1.append(swap(part1_v.at[1], recv1_v.at[1], 1))
    hidden_loads = load_hidden(5)
    w2_load.wait()
    act_grad_stage(0)
    act_grad_stage(1)
    for copy in hidden_loads:
        copy.wait()
    swaps1[0].wait_recv()
    second_stage(0)
    swaps3 = [swap(part3_v.at[0], recv3_v.at[0], 2)]
    branch_stage(0)
    swaps2 = [swap(part2_v.at[0], recv2_v.at[0], 4)]
    swaps1[1].wait_recv()
    second_stage(1)
    swaps3.append(swap(part3_v.at[1], recv3_v.at[1], 3))
    reloads = load_attention(7)
    left_side(lambda c: bl_v[c])
    for u in range(3):
        hidden_unit(u, act_v)
    advance(0, 1)
    left_side(lambda c: e2_v[c])
    hidden_unit(3, low_v)
    advance(1, 1)
    hidden_unit(4, low_v)
    advance(2, 1)
    hidden_unit(5, low_v)
    branch_stage_left = 1
    swaps3[0].wait_recv()
    branch_stage(branch_stage_left)
    advance(0, 2)
    third_stage(0)
    swaps4 = [swap(part3_v.at[0], recv4_v.at[0], 6)]
    advance(3, 1)
    advance(1, 2)
    advance(2, 2)
    swaps2.append(swap(part2_v.at[1], recv2_v.at[1], 5))
    swaps3[1].wait_recv()
    third_stage(1)
    swaps4.append(swap(part3_v.at[1], recv4_v.at[1], 7))
    advance(4, 1)
    advance(0, 3)
    advance(1, 3)
    advance(2, 3)
    advance(3, 2)
    left_side(lambda c: e1_v[c])
    for s in range(3):
        weight_unit(
            6 + s, lambda c, low, size, s=s: act_v[c, :, s * padded + low : s * padded + low + size]
        )
        if s == 0:
            advance(5, 1)
            advance(4, 2)
            advance(0, 4)
            advance(1, 4)
        elif s == 1:
            advance(6, 1)
            advance(2, 4)
    left_side(lambda c: low_v[c, :, :width])
    advance(5, 2)
    weight_unit(9, lambda c, low, size: mixed_v[c, :, low : low + size])
    advance(7, 1)
    advance(3, 3)
    swaps2[0].wait_recv()
    writes = [output_stage(0)]
    advance(8, 1)
    advance(4, 3)
    advance(9, 1)
    swaps4[0].wait_recv()
    writes.append(last_stage(0))
    advance(5, 3)
    advance(3, 4)
    writes[0].wait()
    swaps2[1].wait_recv()
    writes.append(output_stage(1))
    swaps4[1].wait_recv()
    writes.append(last_stage(1))
    advance(4, 4)
    advance(6, 2)
    advance(5, 4)
    advance(8, 2)
    advance(7, 2)
    advance(6, 3)
    advance(8, 3)
    advance(7, 3)
    advance(9, 2)
    advance(6, 4)
    advance(8, 4)
    advance(9, 3)
    advance(7, 4)
    advance(9, 4)
    for copy in writes[1:]:
        copy.wait()
    for copy in swaps1 + swaps2 + swaps4:
        copy.wait_send()
    for (u, stage), copy in started.items():
        if stage > 0 or u >= 7:
            copy.wait_send()


def pair_swap(values, axis, bit, size):
    return lax.ppermute(values, axis, [(i, i ^ bit) for i in range(size)])


def fits(mesh):
    return mesh.shape["mp"] == 2 and mesh.shape["dp"] == 16


def fast_body(
    latents,
    conditioning,
    clip_mask,
    qkv_weight,
    qv_bias,
    proj_weight,
    proj_bias,
    fc1_weight,
    fc1_bias,
    fc2_weight,
    fc2_bias,
    ada_weight,
    ada_bias,
    out_cotangent,
):
    frames, patches, width = latents.shape[1:]
    local = qkv_weight.shape[2]
    padded = -(-local // 128) * 128
    ff = fc1_weight.shape[1]
    dp = lax.axis_size("dp")
    tokens = frames * patches // CHUNKS
    row = lax.axis_index("mp")
    place = lax.axis_index("dp")
    block = width // dp

    scaled = jax.nn.silu(conditioning)
    scaled_low = bf16(scaled)
    mod_local = dot(scaled_low, ada_weight) + f32(ada_bias)
    mod_other = pair_swap(mod_local, "mp", 1, 2)
    modulation = jnp.where(
        row == 0,
        jnp.concatenate([mod_local, mod_other], axis=1),
        jnp.concatenate([mod_other, mod_local], axis=1),
    ).reshape(6, width)
    mask_value = f32(clip_mask[0])
    vec = jnp.stack(
        [
            modulation[0],
            1.0 + modulation[1],
            mask_value * modulation[2],
            modulation[3],
            1.0 + modulation[4],
            modulation[5],
            f32(proj_bias),
            f32(fc2_bias),
        ]
    )
    gate_one, gate_two = vec[2], vec[5]
    qkv_rows = jnp.transpose(qkv_weight, (1, 2, 0))
    bias_rows = jnp.stack([f32(qv_bias[0]), jnp.zeros((local,), jnp.float32), f32(qv_bias[1])])
    hidden_bias = f32(fc1_bias)[None, :]

    def struct(*shape, dtype=jnp.float32):
        return jax.ShapeDtypeStruct(shape, dtype)

    def low(*shape):
        return pltpu.VMEM(shape, jnp.bfloat16)

    planes, third = dp // 2, ff // 3
    outs = [
        (struct(*latents.shape), ANY),
        (struct(*latents.shape), ANY),
        (struct(block, ff), VMEM),
        (struct(block, ff), VMEM),
        (struct(4, block, padded), VMEM),
        (struct(8, width), VMEM),
        (struct(1, ff), VMEM),
        (struct(3, local), VMEM),
    ]
    by_token = low(CHUNKS, tokens, width)
    results = pl.pallas_call(
        block_kernel,
        in_specs=[VMEM] * 5 + [ANY] * 4,
        out_specs=[spec for _, spec in outs],
        out_shape=[shape for shape, _ in outs],
        scratch_shapes=[
            low(4 * local, width),
            low(ff, width),
            by_token,
            low(CHUNKS, 3, tokens, local),
            low(CHUNKS, tokens, padded),
            by_token,
            low(CHUNKS, tokens, ff),
            low(CHUNKS, tokens, ff),
            by_token,
            *[by_token] * 7,
            pltpu.VMEM((CHUNKS, frames, patches // CHUNKS, width), jnp.float32),
            pltpu.VMEM((frames, patches // CHUNKS, width), jnp.float32),
            low(width, CHUNKS * tokens),
            pltpu.VMEM((dp, block, TILE), jnp.float32),
            low(6, planes, block, third),
            low(4, planes, block, padded),
            low(6, planes - 1, block, third),
            low(4, planes - 1, block, padded),
            low(3, planes, block, third),
            low(3, planes, block, third),
            pltpu.SemaphoreType.DMA((15,)),
            pltpu.SemaphoreType.DMA((8,)),
            pltpu.SemaphoreType.DMA((8,)),
            pltpu.SemaphoreType.DMA((10, 4)),
            pltpu.SemaphoreType.DMA((10, 4)),
            pltpu.SemaphoreType.REGULAR((3,)),
        ],
        compiler_params=pltpu.CompilerParams(
            collective_id=0, has_side_effects=True, vmem_limit_bytes=67043328
        ),
    )(
        latents,
        out_cotangent,
        vec,
        bias_rows,
        hidden_bias,
        qkv_rows,
        proj_weight,
        fc1_weight,
        fc2_weight,
    )
    output, grad_latents, fc2_total, fc1_total, rest, stats, hidden_sum, qkv_sums = results
    rest = rest[:, :, :local]

    grad_modulation = jnp.concatenate(
        [
            stats[4],
            stats[5],
            mask_value * stats[2],
            stats[0],
            stats[1],
            stats[6],
        ]
    )
    local_cols = ada_weight.shape[1]
    grad_mod_local = lax.dynamic_slice_in_dim(grad_modulation, row * local_cols, local_cols)
    modulation_low = bf16(grad_mod_local)[None, :]
    scaled_part = dot(modulation_low, ada_weight, NT)
    grad_scaled = scaled_part + pair_swap(scaled_part, "mp", 1, 2)
    grad_cond = jax.vjp(jax.nn.silu, conditioning)[1](grad_scaled)[0]

    pieces = [
        grad_mod_local,
        f32(scaled_low[0]),
        qkv_sums[0],
        qkv_sums[2],
        gate_one * stats[3],
        hidden_sum[0],
        gate_two * stats[7],
    ]
    gathered = lax.all_gather(jnp.concatenate(pieces), "dp", axis=0)
    ends = [0]
    for piece in pieces:
        ends.append(ends[-1] + piece.shape[0])
    items_mod = gathered[:, : ends[1]]
    items_scaled = gathered[:, ends[1] : ends[2]]
    sums = jnp.sum(gathered, axis=0)
    mine = lax.dynamic_slice_in_dim(items_scaled, place * block, block, axis=1)
    grad_ada = dot(bf16(mine), bf16(items_mod), TN)
    qv_total = sums[ends[2] : ends[4]].reshape(2, local)
    return (
        output,
        grad_latents,
        grad_cond,
        jnp.transpose(rest[:3], (1, 0, 2)),
        qv_total,
        rest[3].T,
        sums[ends[4] : ends[5]],
        fc1_total,
        sums[ends[5] : ends[6]],
        fc2_total.T,
        sums[ends[6] : ends[7]],
        grad_ada,
        sums[: ends[1]],
    )


def solution(mesh):
    body = fast_body if fits(mesh) else general_body
    return jax.shard_map(
        body,
        mesh=mesh,
        in_specs=(
            P("dp", None, None, None),
            P("dp", None),
            P("dp"),
            P(None, None, "mp"),
            P(None, "mp"),
            P("mp", None),
            P(),
            P(None, "mp"),
            P("mp"),
            P("mp", None),
            P(),
            P(None, "mp"),
            P("mp"),
            P("dp", None, None, None),
        ),
        out_specs=(
            P("dp", None, None, None),
            P("dp", None, None, None),
            P("dp", None),
            P("dp", None, "mp"),
            P(None, "mp"),
            P("mp", "dp"),
            P(),
            P("dp", "mp"),
            P("mp"),
            P("mp", "dp"),
            P(),
            P("dp", "mp"),
            P("mp"),
        ),
        check_vma=False,
    )
```

```python
from functools import partial

import jax
import jax.numpy as jnp
from jax import lax
from jax.experimental import pallas as pl
from jax.experimental.pallas import tpu as pltpu
from jax.sharding import PartitionSpec as P

HEAD_DIM = 72


def normalize(values):
    centered = values - jnp.mean(values, axis=-1, keepdims=True)
    inverse = lax.rsqrt(jnp.mean(centered * centered, axis=-1, keepdims=True) + 1e-06)
    return (centered * inverse, inverse)


def norm_back(grad_normed, normed, inverse):
    first = jnp.mean(grad_normed, axis=-1, keepdims=True)
    second = jnp.mean(grad_normed * normed, axis=-1, keepdims=True)
    return inverse * (grad_normed - first - normed * second)


def general_body(
    latents,
    conditioning,
    clip_mask,
    qkv_weight,
    qv_bias,
    proj_weight,
    proj_bias,
    fc1_weight,
    fc1_bias,
    fc2_weight,
    fc2_bias,
    ada_weight,
    ada_bias,
    out_cotangent,
):
    frames = latents.shape[1]
    patches = latents.shape[2]
    width = latents.shape[3]
    tok_count = frames * patches
    local_width = qkv_weight.shape[2]
    local_heads = local_width // HEAD_DIM
    factor = HEAD_DIM ** (-0.5)
    stream = latents.reshape(tok_count, width).astype(jnp.float32)
    scaled = jax.nn.silu(conditioning)
    scaled_low = scaled.astype(jnp.bfloat16)
    mod_local = jnp.dot(
        scaled_low, ada_weight, preferred_element_type=jnp.float32
    ) + ada_bias.astype(jnp.float32)
    modulation = lax.all_gather(mod_local, "mp", axis=1, tiled=True).reshape(6, width)
    shift_one = modulation[0]
    scale_one = modulation[1]
    gate_one = modulation[2]
    shift_two = modulation[3]
    scale_two = modulation[4]
    gate_two = modulation[5]
    is_clip = clip_mask[0] > 0
    mask_value = clip_mask[0].astype(jnp.float32)
    normed_one, inverse_one = normalize(stream)
    entry_one = (normed_one * (1.0 + scale_one) + shift_one).astype(jnp.bfloat16)
    qkv_flat = qkv_weight.reshape(width, 3 * local_width)
    bias_rows = qv_bias.astype(jnp.float32)
    bias_full = jnp.stack([bias_rows[0], jnp.zeros_like(bias_rows[0]), bias_rows[1]]).reshape(
        3 * local_width
    )

    def split_heads(projected):
        parts = projected.reshape(frames, patches, 3, local_heads, HEAD_DIM)
        return (parts[:, :, 0], parts[:, :, 1], parts[:, :, 2])

    def softmax_weights(query, keys):
        scores = (
            jnp.einsum("fphd,gphd->phfg", query, keys, preferred_element_type=jnp.float32) * factor
        )
        return jax.nn.softmax(scores, axis=-1)

    def attn_forward(entry):
        projected = (
            jnp.dot(entry, qkv_flat, preferred_element_type=jnp.float32) + bias_full
        ).astype(jnp.bfloat16)
        query, keys, values = split_heads(projected)
        weights = softmax_weights(query, keys)
        mixed = jnp.einsum(
            "phfg,gphd->fphd",
            weights.astype(jnp.bfloat16),
            values,
            preferred_element_type=jnp.float32,
        )
        mixed = mixed.astype(jnp.bfloat16).reshape(tok_count, local_width)
        partial_out = jnp.dot(mixed, proj_weight, preferred_element_type=jnp.float32)
        return (partial_out, projected, mixed)

    def attn_skip(entry):
        return (
            jnp.zeros((tok_count, width), jnp.float32),
            jnp.zeros((tok_count, 3 * local_width), jnp.bfloat16),
            jnp.zeros((tok_count, local_width), jnp.bfloat16),
        )

    partial_out, projected, mixed = lax.cond(is_clip, attn_forward, attn_skip, entry_one)
    attention = lax.psum(partial_out.astype(jnp.bfloat16), "mp").astype(
        jnp.float32
    ) + proj_bias.astype(jnp.float32)
    middle = stream + mask_value * gate_one * attention
    normed_two, inverse_two = normalize(middle)
    entry_two = (normed_two * (1.0 + scale_two) + shift_two).astype(jnp.bfloat16)
    hidden = jnp.dot(entry_two, fc1_weight, preferred_element_type=jnp.float32) + fc1_bias.astype(
        jnp.float32
    )
    activated = jax.nn.gelu(hidden, approximate=True).astype(jnp.bfloat16)
    branch_part = jnp.dot(activated, fc2_weight, preferred_element_type=jnp.float32)
    branch = lax.psum(branch_part.astype(jnp.bfloat16), "mp").astype(jnp.float32) + fc2_bias.astype(
        jnp.float32
    )
    output = middle + gate_two * branch
    grad_out = out_cotangent.reshape(tok_count, width).astype(jnp.float32)
    grad_branch = gate_two * grad_out
    grad_fc2_bias = jnp.sum(grad_branch, axis=0)
    branch_low = grad_branch.astype(jnp.bfloat16)
    grad_fc2 = jnp.einsum("ti,tj->ij", activated, branch_low, preferred_element_type=jnp.float32)
    grad_act = jnp.einsum("tj,ij->ti", branch_low, fc2_weight, preferred_element_type=jnp.float32)
    grad_hidden = jax.vjp(partial(jax.nn.gelu, approximate=True), hidden)[1](grad_act)[0]
    grad_fc1_bias = jnp.sum(grad_hidden, axis=0)
    hidden_low = grad_hidden.astype(jnp.bfloat16)
    grad_fc1 = jnp.einsum("ti,tj->ij", entry_two, hidden_low, preferred_element_type=jnp.float32)
    entry_two_part = jnp.einsum(
        "tj,ij->ti", hidden_low, fc1_weight, preferred_element_type=jnp.float32
    )
    grad_entry_two = lax.psum(entry_two_part.astype(jnp.bfloat16), "mp").astype(jnp.float32)
    grad_gate_two = jnp.sum(grad_out * branch, axis=0)
    grad_shift_two = jnp.sum(grad_entry_two, axis=0)
    grad_scale_two = jnp.sum(grad_entry_two * normed_two, axis=0)
    grad_middle = grad_out + norm_back(grad_entry_two * (1.0 + scale_two), normed_two, inverse_two)
    grad_gate_one = mask_value * jnp.sum(grad_middle * attention, axis=0)
    grad_attention = mask_value * gate_one * grad_middle
    grad_proj_bias = jnp.sum(grad_attention, axis=0)
    attention_low = grad_attention.astype(jnp.bfloat16)

    def attn_backward(operands):
        grad_low, kept_projected, kept_mixed = operands
        grad_proj = jnp.einsum(
            "ti,tj->ij", kept_mixed, grad_low, preferred_element_type=jnp.float32
        )
        grad_mixed = jnp.einsum(
            "tj,ij->ti", grad_low, proj_weight, preferred_element_type=jnp.float32
        )
        grad_mixed = grad_mixed.astype(jnp.bfloat16).reshape(frames, patches, local_heads, HEAD_DIM)
        query, keys, values = split_heads(kept_projected)
        weights = softmax_weights(query, keys)
        grad_values = jnp.einsum(
            "phfg,fphd->gphd",
            weights.astype(jnp.bfloat16),
            grad_mixed,
            preferred_element_type=jnp.float32,
        )
        grad_weights = jnp.einsum(
            "fphd,gphd->phfg", grad_mixed, values, preferred_element_type=jnp.float32
        )
        grad_scores = weights * (
            grad_weights - jnp.sum(weights * grad_weights, axis=-1, keepdims=True)
        )
        grad_scores = grad_scores.astype(jnp.bfloat16)
        grad_query = (
            jnp.einsum("phfg,gphd->fphd", grad_scores, keys, preferred_element_type=jnp.float32)
            * factor
        )
        grad_keys = (
            jnp.einsum("phfg,fphd->gphd", grad_scores, query, preferred_element_type=jnp.float32)
            * factor
        )
        grad_all = (
            jnp.stack([grad_query, grad_keys, grad_values], axis=2)
            .astype(jnp.bfloat16)
            .reshape(tok_count, 3 * local_width)
        )
        column_sums = jnp.sum(grad_all.astype(jnp.float32), axis=0).reshape(3, local_width)
        grad_qv = jnp.stack([column_sums[0], column_sums[2]])
        grad_qkv = jnp.einsum(
            "ti,tj->ij", entry_one, grad_all, preferred_element_type=jnp.float32
        ).reshape(width, 3, local_width)
        grad_entry = jnp.einsum("tj,ij->ti", grad_all, qkv_flat, preferred_element_type=jnp.float32)
        return (grad_proj, grad_qv, grad_qkv, grad_entry)

    def skip_backward(operands):
        return (
            jnp.zeros((local_width, width), jnp.float32),
            jnp.zeros((2, local_width), jnp.float32),
            jnp.zeros((width, 3, local_width), jnp.float32),
            jnp.zeros((tok_count, width), jnp.float32),
        )

    grad_proj, grad_qv, grad_qkv, entry_one_part = lax.cond(
        is_clip, attn_backward, skip_backward, (attention_low, projected, mixed)
    )
    grad_entry_one = lax.psum(entry_one_part.astype(jnp.bfloat16), "mp").astype(jnp.float32)
    grad_shift_one = jnp.sum(grad_entry_one, axis=0)
    grad_scale_one = jnp.sum(grad_entry_one * normed_one, axis=0)
    grad_latents = grad_middle + norm_back(
        grad_entry_one * (1.0 + scale_one), normed_one, inverse_one
    )
    grad_modulation = jnp.concatenate(
        [
            grad_shift_one,
            grad_scale_one,
            grad_gate_one,
            grad_shift_two,
            grad_scale_two,
            grad_gate_two,
        ]
    )
    local_cols = ada_weight.shape[1]
    grad_mod_local = lax.dynamic_slice_in_dim(
        grad_modulation, lax.axis_index("mp") * local_cols, local_cols
    )[None, :]
    grad_ada_bias = jnp.sum(grad_mod_local, axis=0)
    modulation_low = grad_mod_local.astype(jnp.bfloat16)
    scaled_part = jnp.einsum(
        "tj,ij->ti", modulation_low, ada_weight, preferred_element_type=jnp.float32
    )
    grad_scaled = lax.psum(scaled_part, "mp")
    grad_cond = jax.vjp(jax.nn.silu, conditioning)[1](grad_scaled)[0]
    ada_term = jnp.einsum(
        "ti,tj->ij", scaled_low, modulation_low, preferred_element_type=jnp.float32
    )
    grad_ada = lax.psum_scatter(
        ada_term.astype(jnp.bfloat16), "dp", scatter_dimension=0, tiled=True
    ).astype(jnp.float32)
    qkv_total, proj_total, fc1_total, fc2_total = (
        lax.psum_scatter(
            grad_qkv.astype(jnp.bfloat16), "dp", scatter_dimension=0, tiled=True
        ).astype(jnp.float32),
        lax.psum_scatter(
            grad_proj.astype(jnp.bfloat16), "dp", scatter_dimension=1, tiled=True
        ).astype(jnp.float32),
        lax.psum_scatter(
            grad_fc1.astype(jnp.bfloat16), "dp", scatter_dimension=0, tiled=True
        ).astype(jnp.float32),
        lax.psum_scatter(
            grad_fc2.astype(jnp.bfloat16), "dp", scatter_dimension=1, tiled=True
        ).astype(jnp.float32),
    )
    qv_total, proj_bias_total, fc1_bias_total, fc2_bias_total, ada_bias_total = lax.psum(
        (grad_qv, grad_proj_bias, grad_fc1_bias, grad_fc2_bias, grad_ada_bias), "dp"
    )
    return (
        output.reshape(latents.shape),
        grad_latents.reshape(latents.shape),
        grad_cond,
        qkv_total,
        qv_total,
        proj_total,
        proj_bias_total,
        fc1_total,
        fc1_bias_total,
        fc2_total,
        fc2_bias_total,
        grad_ada,
        ada_bias_total,
    )


NT = (((1,), (1,)), ((), ()))
TN = (((0,), (0,)), ((), ()))
CHUNKS = 2
TILE = 256
GELU_A = 0.7978845608028654
GELU_B = 0.044715
VMEM = pl.BlockSpec(memory_space=pltpu.VMEM)
ANY = pl.BlockSpec(memory_space=pl.ANY)
ORDERS = ((1, 2, 3), (1, 2, 3), (2, 1, 3), (1, 2, 3), (1, 2, 3), (1, 2, 3), (1, 2, 3), (1, 2, 3), (2, 1, 3), (1, 2, 3))


def f32(values):
    return values.astype(jnp.float32)


def bf16(values):
    return values.astype(jnp.bfloat16)


def dot(left, right, dims=(((1,), (0,)), ((), ()))):
    return lax.dot_general(left, right, dims, preferred_element_type=jnp.float32)


def repeat(count, visit):
    def at(i, carry):
        visit(i)
        return carry

    lax.fori_loop(0, count, at, 0)


def head_spans(width):
    spans = []
    for head in range(width // HEAD_DIM):
        first, last = head * HEAD_DIM, (head + 1) * HEAD_DIM
        low = first // 128 * 128
        high = min(-(-last // 128) * 128, width)
        spans.append((first, last, low, high))
    return spans


def lane_mask(first, last, low, high):
    lane = lax.broadcasted_iota(jnp.int32, (1, high - low), 1) + low
    return (lane >= first) & (lane < last)


def same_patch(tokens, per_frame):
    row = lax.broadcasted_iota(jnp.int32, (tokens, tokens), 0)
    col = lax.broadcasted_iota(jnp.int32, (tokens, tokens), 1)
    return (row % per_frame) == (col % per_frame)


def attention_weights(query, keys, allowed):
    scores = dot(query, keys, NT) * (HEAD_DIM ** (-0.5))
    scores = jnp.where(allowed, scores, -1e30)
    grown = jnp.exp(scores - jnp.max(scores, axis=-1, keepdims=True))
    return grown / jnp.sum(grown, axis=-1, keepdims=True)


def column_blocks(width, block):
    return [(low, min(block, width - low)) for low in range(0, width, block)]


def block_kernel(
    lat_ref,
    dy_ref,
    cond_ref,
    mask_ref,
    small_ref,
    w_hbm,
    pw_hbm,
    w1_hbm,
    w2_hbm,
    ada_hbm,
    out_hbm,
    glat_hbm,
    gcond_ref,
    gqkv_ref,
    gqv_ref,
    gproj_ref,
    gpb_ref,
    rs1_ref,
    gb1_ref,
    rs2_ref,
    gb2_ref,
    gada_ref,
    gadab_ref,
    vec_ref,
    stat_ref,
    hsum_ref,
    qsum_ref,
    b1_v,
    modx_v,
    spx_v,
    gath_v,
    wide_v,
    w2_v,
    e1_v,
    proj_v,
    mixed_v,
    e2_v,
    act_v,
    low_v,
    bl_v,
    part1_v,
    recv1_v,
    part2_v,
    recv2_v,
    part3_v,
    recv3_v,
    recv4_v,
    gmid_v,
    stage_v,
    left_v,
    tile_v,
    keep_a,
    keep_b,
    later_a,
    later_b,
    send0_v,
    recv0_v,
    load_sem,
    ada_sem,
    y_send,
    y_recv,
    rs_send,
    rs_recv,
    g_send,
    g_recv,
    credit,
):
    frames, patches, width = lat_ref.shape[1:]
    per_frame = patches // CHUNKS
    tokens = frames * per_frame
    local = proj_v.shape[3]
    padded = mixed_v.shape[2]
    ff = act_v.shape[2]
    planes, rows = send0_v.shape[1], send0_v.shape[2]
    place = lax.axis_index("dp")
    across = 1 - lax.axis_index("mp")
    bit_of = [(place // (1 << b)) % 2 for b in range(4)]
    partner = [place + (1 - 2 * bit_of[b]) * (1 << b) for b in range(4)]
    core = bit_of[0]

    barrier = pltpu.get_barrier_semaphore()
    pl.semaphore_signal(barrier, inc=1, device_id={"mp": across}, device_id_type=pl.DeviceIdType.MESH)
    for other in partner:
        pl.semaphore_signal(barrier, inc=1, device_id={"dp": other}, device_id_type=pl.DeviceIdType.MESH)

    def load(source, target, index):
        copy = pltpu.make_async_copy(source, target, load_sem.at[index])
        copy.start()
        return copy

    def load_attention(index):
        copies = [
            load(w_hbm.at[s], wide_v.at[s * local : (s + 1) * local, :], index + s) for s in range(3)
        ]
        return copies + [load(pw_hbm, wide_v.at[3 * local :, :], index + 3)]

    def load_hidden(index):
        return [
            load(w1_hbm.at[:, i * width : (i + 1) * width], wide_v.at[i * width : (i + 1) * width, :], index + i)
            for i in range(2)
        ]

    deep = act_v.shape[1]
    ada_tail = [
        (low * deep, min(deep, width - low * deep), place_ref)
        for low, place_ref in enumerate(
            (
                act_v.at[0, :, :width],
                act_v.at[0, :, width:],
                act_v.at[1, :, :width],
                act_v.at[1, :, width:],
                low_v.at[0, :, :width],
            )
        )
    ]

    def load_ada():
        pairs = [
            (ada_hbm.at[:, i * width : (i + 1) * width], w2_v.at[i * width : (i + 1) * width, :])
            for i in range(2)
        ]
        for low, size, target in ada_tail:
            pairs.append(
                (ada_hbm.at[low : low + size, 2 * width :], target.at[0:size, :])
            )
        copies = []
        for i, (source, target) in enumerate(pairs):
            copies.append(pltpu.make_async_copy(source, target, ada_sem.at[i]))
            copies[-1].start()
        return copies

    first_ada = load_ada()
    attention_loads = load_attention(0)
    stat_ref[...] = jnp.zeros_like(stat_ref)
    for i in range(ff // width):
        b1_v[:, i * width : (i + 1) * width] = small_ref[5 + i : 6 + i, :]
    first_half = lax.axis_index("mp") == 0
    masked = mask_ref[0].astype(jnp.float32)
    SHIFT, PB, B2, B1, QV = 0, 3, 4, 5, 7

    def tall(values):
        return bf16(jnp.broadcast_to(values, (8, values.shape[-1])))

    def modulate():
        sigmoid = 1.0 / (1.0 + jnp.exp(-cond_ref[...]))
        scaled = tall(cond_ref[...] * sigmoid)
        for copy in first_ada:
            copy.wait()
        for i in range(2):
            found = dot(scaled, w2_v[i * width : (i + 1) * width, :])
            modx_v[0, i : i + 1, :] = found[0:1] + small_ref[SHIFT + i : SHIFT + i + 1, :]
        total = small_ref[SHIFT + 2 : SHIFT + 3, :]
        for low, size, target in ada_tail:
            total += dot(scaled[:, low : low + size], target[0:size, :])[0:1]
        modx_v[0, 2:3, :] = total

    def place_modulation():
        def both(i):
            mine, theirs = modx_v[0, i : i + 1, :], modx_v[1, i : i + 1, :]
            return jnp.where(first_half, mine, theirs), jnp.where(first_half, theirs, mine)

        (shift_one, shift_two), (scale_one, scale_two), (gate_one, gate_two) = map(both, range(3))
        vec_ref[0:1, :] = shift_one
        vec_ref[1:2, :] = 1.0 + scale_one
        vec_ref[2:3, :] = masked * gate_one
        vec_ref[3:4, :] = shift_two
        vec_ref[4:5, :] = 1.0 + scale_two
        vec_ref[5:6, :] = gate_two
        vec_ref[6:7, :] = small_ref[PB : PB + 1, :]
        vec_ref[7:8, :] = small_ref[B2 : B2 + 1, :]

    ring = (1, 2, 3, 0)
    slot_bits = [bit_of[b] for b in ring]
    my_slot = sum(v * (1 << i) for i, v in enumerate(slot_bits))

    def vector_rows():
        gath_v[my_slot] = jnp.zeros(gath_v.shape[1:], jnp.float32)
        mine = (stat_ref[4:5, :], stat_ref[5:6, :], masked * stat_ref[2:3, :])
        theirs = (stat_ref[0:1, :], stat_ref[1:2, :], stat_ref[6:7, :])
        for i in range(3):
            gath_v[my_slot, i : i + 1, :] = jnp.where(first_half, mine[i], theirs[i])
        sigmoid = 1.0 / (1.0 + jnp.exp(-cond_ref[...]))
        gath_v[my_slot, 3:4, :] = f32(bf16(cond_ref[...] * sigmoid))
        gath_v[my_slot, 4:5, :] = vec_ref[2:3, :] * stat_ref[3:4, :]
        gath_v[my_slot, 5:6, :] = vec_ref[5:6, :] * stat_ref[7:8, :]
        gath_v[my_slot, 6:7, :] = hsum_ref[:, :width]
        gath_v[my_slot, 7:8, :] = hsum_ref[:, width:]
        gath_v[my_slot, 8:9, :local] = qsum_ref[0:1, :]
        gath_v[my_slot, 9:10, :local] = qsum_ref[2:3, :]

    def gather_step(k):
        held = sum(slot_bits[i] * (1 << i) for i in range(k, 4))
        at = pl.ds(held, 1 << k)
        copy = pltpu.make_async_remote_copy(
            src_ref=gath_v.at[at],
            dst_ref=gath_v.at[at],
            send_sem=g_send.at[k],
            recv_sem=g_recv.at[k],
            device_id={"dp": partner[ring[k]]},
            device_id_type=pl.DeviceIdType.MESH,
        )
        copy.start()
        return copy

    def scaled_back():
        rows_of = [tall(gath_v[my_slot, i : i + 1, :]) for i in range(3)]
        for copy in second_ada:
            copy.wait()
        spx_v[0] = dot(rows_of[0], w2_v[:width, :], NT) + dot(rows_of[1], w2_v[width:, :], NT)
        for low, size, target in ada_tail:
            spx_v[0, :, low : low + size] += dot(rows_of[2], target[0:size, :], NT)

    def conditioning_out():
        total = spx_v[0, 0:1, :] + spx_v[1, 0:1, :]
        cond = cond_ref[...]
        sigmoid = 1.0 / (1.0 + jnp.exp(-cond))
        gcond_ref[...] = total * sigmoid * (1.0 + cond * (1.0 - sigmoid))

    def vectors_out():
        items = gath_v.shape[0]
        total = gath_v[0]
        for i in range(1, items):
            total += gath_v[i]
        gadab_ref[...] = total[0:3]
        gpb_ref[...] = total[4:5]
        gb2_ref[...] = total[5:6]
        gb1_ref[...] = total[6:8]
        gqv_ref[...] = total[8:10, :local]

        def column(row):
            return bf16(jnp.concatenate([gath_v[i, row : row + 1, :] for i in range(items)], axis=0))

        one = lax.broadcasted_iota(jnp.int32, (rows, width), 1)
        down = lax.broadcasted_iota(jnp.int32, (rows, width), 0)
        chosen = jnp.where(one == down + place * rows, 1.0, 0.0).astype(jnp.bfloat16)
        block = bf16(dot(chosen, column(3), NT))
        for i in range(3):
            gada_ref[:, i * width : (i + 1) * width] = dot(block, column(i))

    step = 2 * per_frame

    def token_rows(ref, chunk, i):
        block = ref[0, pl.ds(2 * i, 2), chunk * per_frame : (chunk + 1) * per_frame, :]
        return f32(block).reshape(step, width)

    def over_rows(visit):
        repeat(tokens // step, lambda i: visit(i, pl.ds(pl.multiple_of(i * step, step), step)))

    def swap(source, target, index):
        copy = pltpu.make_async_remote_copy(
            src_ref=source,
            dst_ref=target,
            send_sem=y_send.at[index],
            recv_sem=y_recv.at[index],
            device_id={"mp": across},
            device_id_type=pl.DeviceIdType.MESH,
        )
        copy.start()
        return copy

    def add_stat(row, values):
        stat_ref[row : row + 1, :] += jnp.sum(values, axis=0, keepdims=True)

    def bias_of(s):
        if s == 1:
            return jnp.zeros((1, local), jnp.float32)
        return small_ref[QV + s // 2 : QV + s // 2 + 1, :local]

    allowed = same_patch(tokens, per_frame)
    spans = head_spans(local)
    factor = HEAD_DIM ** (-0.5)

    def first_stage(c):
        def enter(i, at):
            normed, _ = normalize(token_rows(lat_ref, c, i))
            e1_v[c, at, :] = bf16(normed * vec_ref[1:2, :] + vec_ref[0:1, :])

        over_rows(enter)
        for s in range(3):
            if c == 0:
                attention_loads[s].wait()
            weight = wide_v[s * local : (s + 1) * local, :]
            proj_v[c, s] = bf16(dot(e1_v[c], weight, NT) + bias_of(s))
        mixed_v[c, :, padded - 128 :] = jnp.zeros((tokens, 128), jnp.bfloat16)
        for first, last, low, high in spans:
            mask = lane_mask(first, last, low, high)
            query = jnp.where(mask, proj_v[c, 0, :, low:high], 0)
            weights = attention_weights(query, proj_v[c, 1, :, low:high], allowed)
            mixed = dot(bf16(weights), proj_v[c, 2, :, low:high])
            mixed_v[c, :, low:high] = bf16(jnp.where(mask, mixed, f32(mixed_v[c, :, low:high])))
        if c == 0:
            attention_loads[3].wait()
        part1_v[c] = bf16(dot(mixed_v[c, :, :local], wide_v[3 * local :, :]))

    def act_grad_stage(c):
        def enter(i, at):
            grad = token_rows(dy_ref, c, i)
            add_stat(7, grad)
            bl_v[c, at, :] = bf16(grad * vec_ref[5:6, :])

        over_rows(enter)

        def columns(j):
            at = pl.ds(pl.multiple_of(j * TILE, TILE), TILE)
            low_v[c, :, at] = bf16(dot(bl_v[c], w2_v[at, :], NT))

        repeat(ff // TILE, columns)

    def middle_rows(c, i, at):
        attention = f32(part1_v[c, at, :]) + f32(recv1_v[c, at, :]) + vec_ref[6:7, :]
        return attention, token_rows(lat_ref, c, i) + vec_ref[2:3, :] * attention

    def second_stage(c):
        def enter(i, at):
            _, middle = middle_rows(c, i, at)
            normed, _ = normalize(middle)
            e2_v[c, at, :] = bf16(normed * vec_ref[4:5, :] + vec_ref[3:4, :])

        over_rows(enter)

        def half(i):
            base = pl.multiple_of(i * width, width)
            for low, size in column_blocks(width, TILE):
                at = pl.ds(pl.multiple_of(base + low, 128), size)
                hidden = dot(e2_v[c], wide_v[pl.ds(base, width), low : low + size]) + b1_v[:, at]
                square = hidden * hidden
                bent = jnp.tanh(GELU_A * hidden * (1.0 + GELU_B * square))
                gate = 0.5 * (1.0 + bent)
                act_v[c, :, at] = bf16(hidden * gate)
                slope = gate + 0.5 * hidden * (1.0 - bent * bent) * (
                    GELU_A * (1.0 + 3.0 * GELU_B * square)
                )
                grad_hidden = f32(low_v[c, :, at]) * slope
                found = jnp.sum(grad_hidden, axis=0, keepdims=True)
                hsum_ref[:, at] = found if c == 0 else hsum_ref[:, at] + found
                low_v[c, :, at] = bf16(grad_hidden)

        repeat(ff // width, half)
        for low, size in column_blocks(width, 2 * TILE):
            total = dot(low_v[c, :, :width], wide_v[low : low + size, :], NT)
            total += dot(low_v[c, :, width:], wide_v[width + low : width + low + size, :], NT)
            part3_v[c, :, low : low + size] = bf16(total)

    def branch_stage(c):
        for low, size in column_blocks(width, 2 * TILE):
            part2_v[c, :, low : low + size] = bf16(dot(act_v[c], w2_v[:, low : low + size]))

    def third_stage(c):
        grads = [act_v.at[c, :, s * padded : (s + 1) * padded] for s in range(3)]
        alow = low_v.at[c, :, :width]
        mixed_grad = low_v.at[c, :, width : width + padded]

        def enter(i, at):
            attention, middle = middle_rows(c, i, at)
            normed, inverse = normalize(middle)
            grad_entry = f32(part3_v[c, at, :]) + f32(recv3_v[c, at, :])
            add_stat(0, grad_entry)
            add_stat(1, grad_entry * normed)
            grad_middle = token_rows(dy_ref, c, i) + norm_back(
                grad_entry * vec_ref[4:5, :], normed, inverse
            )
            add_stat(2, grad_middle * attention)
            add_stat(3, grad_middle)
            gmid_v[c, pl.ds(2 * i, 2)] = grad_middle.reshape(2, per_frame, width)
            alow[at, :] = bf16(vec_ref[2:3, :] * grad_middle)

        over_rows(enter)
        if c == 0:
            reloads[3].wait()
        mixed_grad[:, :local] = bf16(dot(alow[...], wide_v[3 * local :, :], NT))
        for first, last, low, high in spans:
            mask = lane_mask(first, last, low, high)
            query, keys, values = (proj_v[c, s, :, low:high] for s in range(3))
            grad_mixed = mixed_grad[:, low:high]
            weights = attention_weights(jnp.where(mask, query, 0), keys, allowed)
            grad_weights = dot(jnp.where(mask, grad_mixed, 0), values, NT)
            grad_scores = bf16(
                weights * (grad_weights - jnp.sum(weights * grad_weights, axis=-1, keepdims=True))
            )
            found = (
                dot(grad_scores, keys) * factor,
                dot(grad_scores, query, TN) * factor,
                dot(bf16(weights), grad_mixed, TN),
            )
            for s in range(3):
                grads[s][:, low:high] = bf16(jnp.where(mask, found[s], f32(grads[s][:, low:high])))
        for s in range(3):
            if c == 0:
                reloads[s].wait()
            found = jnp.sum(f32(grads[s][:, :local]), axis=0, keepdims=True)
            if c == 0:
                qsum_ref[s : s + 1, :] = found
            else:
                qsum_ref[s : s + 1, :] += found
        swaps3[c].wait_send()
        for low, size in column_blocks(width, 2 * TILE):
            at = slice(low, low + size)
            total = dot(grads[0][:, :local], wide_v[:local, at])
            total += dot(grads[1][:, :local], wide_v[local : 2 * local, at])
            total += dot(grads[2][:, :local], wide_v[2 * local : 3 * local, at])
            part3_v[c, :, at] = bf16(total)

    def last_stage(c):
        def leave(i, at):
            normed, inverse = normalize(token_rows(lat_ref, c, i))
            grad_entry = f32(part3_v[c, at, :]) + f32(recv4_v[c, at, :])
            add_stat(4, grad_entry)
            add_stat(5, grad_entry * normed)
            result = norm_back(grad_entry * vec_ref[1:2, :], normed, inverse)
            gmid_v[c, pl.ds(2 * i, 2)] += result.reshape(2, per_frame, width)

        over_rows(leave)
        return load(
            gmid_v.at[c], glat_hbm.at[0, :, c * per_frame : (c + 1) * per_frame, :], 11 + c
        )

    def output_stage(c):
        def leave(i, at):
            _, middle = middle_rows(c, i, at)
            branch = f32(part2_v[c, at, :]) + f32(recv2_v[c, at, :]) + vec_ref[7:8, :]
            add_stat(6, token_rows(dy_ref, c, i) * branch)
            stage_v[pl.ds(2 * i, 2)] = (middle + vec_ref[5:6, :] * branch).reshape(
                2, per_frame, width
            )

        over_rows(leave)
        return load(stage_v, out_hbm.at[0, :, c * per_frame : (c + 1) * per_frame, :], 13 + c)

    third = send0_v.shape[3]
    started = {}

    def unit_refs(u):
        if u < 6:
            return keep_a.at[u], later_a.at[u], third
        return keep_b.at[u - 6], later_b.at[u - 6], padded

    def left_side(source):
        for c in range(CHUNKS):
            left_v[:, c * tokens : (c + 1) * tokens] = source(c).T

    def weight_unit(u, right):
        keep, _, columns = unit_refs(u)
        slot = u % 3
        if u >= 3:
            started[u - 3, 0].wait_send()
        send = send0_v.at[slot]

        def part(low, size):
            block = jnp.concatenate([right(c, low, size) for c in range(CHUNKS)], axis=0)
            half = width // 2
            for i in range(2):
                found = dot(left_v[i * half : (i + 1) * half, :], block)
                tile_v[i * planes : (i + 1) * planes, :, :size] = found.reshape(planes, rows, size)
            first, second, third_bit = ORDERS[u]
            for j in range(planes):
                even = (j // 4 << first) + (j // 2 % 2 << second) + (j % 2 << third_bit)
                keep[j, :, pl.ds(low, size)] = bf16(tile_v[even + core, :, :size])
                send[j, :, pl.ds(low, size)] = bf16(tile_v[even + 1 - core, :, :size])

        if columns % TILE == 0:
            repeat(columns // TILE, lambda t: part(pl.multiple_of(t * TILE, TILE), TILE))
        else:
            for low, size in column_blocks(columns, TILE):
                part(low, size)
        if u >= 3:
            pl.semaphore_wait(credit.at[slot], 1)
        copy = pltpu.make_async_remote_copy(
            src_ref=send.at[:, :, 0:columns],
            dst_ref=recv0_v.at[slot, :, :, 0:columns],
            send_sem=rs_send.at[u, 0],
            recv_sem=rs_recv.at[u, 0],
            device_id={"dp": partner[0]},
            device_id_type=pl.DeviceIdType.MESH,
        )
        copy.start()
        started[u, 0] = copy

    def advance(u, stage):
        keep, later, columns = unit_refs(u)
        slot = u % 3
        order = ORDERS[u]
        started[u, stage - 1].wait_recv()
        base = sum(bit_of[order[i]] * (4 >> i) for i in range(stage - 1))
        if stage == 1:
            come = recv0_v.at[slot, :, :, 0:columns]
        else:
            come = later.at[(0, 4, 6)[stage - 2] :]
        if stage == 4:
            total = f32(keep[base]) + f32(come[0])
            if u < 3:
                rs2_ref[:, u * third : (u + 1) * third] = total
            elif u < 6:
                rs1_ref[:, (u - 3) * third : (u - 2) * third] = total
            elif u < 9:
                gqkv_ref[u - 6] = total[:, :local]
            else:
                gproj_ref[...] = total[:, :local]
            return
        count = 4 >> (stage - 1)
        mine = bit_of[order[stage - 1]]

        def add(which):
            def one(i):
                at = which * count + i
                keep[base + at] = bf16(f32(keep[base + at]) + f32(come[at]))

            repeat(count, one)

        add(1 - mine)
        other = partner[order[stage - 1]]
        copy = pltpu.make_async_remote_copy(
            src_ref=keep.at[pl.ds(base + (1 - mine) * count, count)],
            dst_ref=later.at[(0, 4, 6)[stage - 1] : (0, 4, 6)[stage - 1] + count],
            send_sem=rs_send.at[u, stage],
            recv_sem=rs_recv.at[u, stage],
            device_id={"dp": other},
            device_id_type=pl.DeviceIdType.MESH,
        )
        copy.start()
        started[u, stage] = copy
        add(mine)
        if stage == 1 and u < 7:
            pl.semaphore_signal(
                credit.at[slot],
                inc=1,
                device_id={"dp": partner[0]},
                device_id_type=pl.DeviceIdType.MESH,
            )

    def hidden_unit(u, right_v):
        weight_unit(u, lambda c, low, size: right_v[c, :, pl.ds((u % 3) * third + low, size)])

    modulate()
    pl.semaphore_wait(barrier, 5)
    mod_swap = swap(modx_v.at[0], modx_v.at[1], 8)
    w2_load = load(w2_hbm, w2_v, 4)
    mod_swap.wait_recv()
    place_modulation()
    first_stage(0)
    swaps1 = [swap(part1_v.at[0], recv1_v.at[0], 0)]
    first_stage(1)
    swaps1.append(swap(part1_v.at[1], recv1_v.at[1], 1))
    hidden_loads = load_hidden(5)
    w2_load.wait()
    act_grad_stage(0)
    act_grad_stage(1)
    for copy in hidden_loads:
        copy.wait()
    swaps1[0].wait_recv()
    second_stage(0)
    swaps3 = [swap(part3_v.at[0], recv3_v.at[0], 2)]
    branch_stage(0)
    swaps2 = [swap(part2_v.at[0], recv2_v.at[0], 4)]
    swaps1[1].wait_recv()
    second_stage(1)
    swaps3.append(swap(part3_v.at[1], recv3_v.at[1], 3))
    reloads = load_attention(7)
    left_side(lambda c: bl_v[c])
    for u in range(3):
        hidden_unit(u, act_v)
    advance(0, 1)
    left_side(lambda c: e2_v[c])
    hidden_unit(3, low_v)
    advance(1, 1)
    hidden_unit(4, low_v)
    advance(2, 1)
    hidden_unit(5, low_v)
    branch_stage_left = 1
    swaps3[0].wait_recv()
    branch_stage(branch_stage_left)
    advance(0, 2)
    third_stage(0)
    swaps4 = [swap(part3_v.at[0], recv4_v.at[0], 6)]
    advance(3, 1)
    advance(1, 2)
    advance(2, 2)
    swaps2.append(swap(part2_v.at[1], recv2_v.at[1], 5))
    swaps3[1].wait_recv()
    third_stage(1)
    swaps4.append(swap(part3_v.at[1], recv4_v.at[1], 7))
    advance(4, 1)
    advance(0, 3)
    advance(1, 3)
    advance(2, 3)
    advance(3, 2)
    left_side(lambda c: e1_v[c])
    for s in range(3):
        weight_unit(
            6 + s, lambda c, low, size, s=s: act_v[c, :, s * padded + low : s * padded + low + size]
        )
        if s == 0:
            advance(5, 1)
            advance(4, 2)
            advance(0, 4)
            advance(1, 4)
        elif s == 1:
            advance(6, 1)
            advance(2, 4)
    left_side(lambda c: low_v[c, :, :width])
    advance(5, 2)
    weight_unit(9, lambda c, low, size: mixed_v[c, :, low : low + size])
    advance(7, 1)
    advance(3, 3)
    swaps2[0].wait_recv()
    writes = [output_stage(0)]
    advance(8, 1)
    advance(4, 3)
    advance(9, 1)
    swaps4[0].wait_recv()
    writes.append(last_stage(0))
    advance(5, 3)
    advance(3, 4)
    writes[0].wait()
    swaps2[1].wait_recv()
    writes.append(output_stage(1))
    swaps4[1].wait_recv()
    writes.append(last_stage(1))
    second_ada = load_ada()
    vector_rows()
    gathers = [gather_step(0)]
    advance(4, 4)
    advance(6, 2)
    scaled_back()
    scaled_swap = swap(spx_v.at[0], spx_v.at[1], 9)
    advance(5, 4)
    gathers[0].wait_recv()
    gathers.append(gather_step(1))
    advance(8, 2)
    advance(7, 2)
    advance(6, 3)
    gathers[1].wait_recv()
    gathers.append(gather_step(2))
    advance(8, 3)
    advance(7, 3)
    advance(9, 2)
    gathers[2].wait_recv()
    gathers.append(gather_step(3))
    scaled_swap.wait_recv()
    conditioning_out()
    advance(6, 4)
    advance(8, 4)
    gathers[3].wait_recv()
    vectors_out()
    advance(9, 3)
    advance(7, 4)
    advance(9, 4)
    for copy in writes[1:]:
        copy.wait()
    for copy in swaps1 + swaps2 + swaps4 + [mod_swap, scaled_swap] + gathers:
        copy.wait_send()
    for (u, stage), copy in started.items():
        if stage > 0 or u >= 7:
            copy.wait_send()


def fits(mesh):
    return mesh.shape["mp"] == 2 and mesh.shape["dp"] == 16


def fast_body(
    latents,
    conditioning,
    clip_mask,
    qkv_weight,
    qv_bias,
    proj_weight,
    proj_bias,
    fc1_weight,
    fc1_bias,
    fc2_weight,
    fc2_bias,
    ada_weight,
    ada_bias,
    out_cotangent,
):
    frames, patches, width = latents.shape[1:]
    local = qkv_weight.shape[2]
    padded = -(-local // 128) * 128
    ff = fc1_weight.shape[1]
    dp = lax.axis_size("dp")
    tokens = frames * patches // CHUNKS
    block = width // dp

    wide = [ada_bias.reshape(3, width), proj_bias[None], fc2_bias[None], fc1_bias.reshape(-1, width)]
    wide.append(jnp.pad(qv_bias, ((0, 0), (0, width - local))))
    small = jnp.concatenate([f32(part) for part in wide], axis=0)
    qkv_rows = jnp.transpose(qkv_weight, (1, 2, 0))

    def struct(*shape, dtype=jnp.float32):
        return jax.ShapeDtypeStruct(shape, dtype)

    def low(*shape):
        return pltpu.VMEM(shape, jnp.bfloat16)

    planes, third = dp // 2, ff // 3
    outs = [
        (struct(*latents.shape), ANY),
        (struct(*latents.shape), ANY),
        (struct(1, width), VMEM),
        (struct(3, block, local), VMEM),
        (struct(2, local), VMEM),
        (struct(block, local), VMEM),
        (struct(1, width), VMEM),
        (struct(block, ff), VMEM),
        (struct(ff // width, width), VMEM),
        (struct(block, ff), VMEM),
        (struct(1, width), VMEM),
        (struct(block, 3 * width), VMEM),
        (struct(3, width), VMEM),
    ]
    by_token = low(CHUNKS, tokens, width)
    results = pl.pallas_call(
        block_kernel,
        in_specs=[VMEM] * 3 + [pl.BlockSpec(memory_space=pltpu.SMEM), VMEM] + [ANY] * 5,
        out_specs=[spec for _, spec in outs],
        out_shape=[shape for shape, _ in outs],
        scratch_shapes=[
            pltpu.VMEM((8, width), jnp.float32),
            pltpu.VMEM((8, width), jnp.float32),
            pltpu.VMEM((1, ff), jnp.float32),
            pltpu.VMEM((3, local), jnp.float32),
            pltpu.VMEM((1, ff), jnp.float32),
            pltpu.VMEM((2, 8, width), jnp.float32),
            pltpu.VMEM((2, 8, width), jnp.float32),
            pltpu.VMEM((dp, 10, width), jnp.float32),
            low(4 * local, width),
            low(ff, width),
            by_token,
            low(CHUNKS, 3, tokens, local),
            low(CHUNKS, tokens, padded),
            by_token,
            low(CHUNKS, tokens, ff),
            low(CHUNKS, tokens, ff),
            by_token,
            *[by_token] * 7,
            pltpu.VMEM((CHUNKS, frames, patches // CHUNKS, width), jnp.float32),
            pltpu.VMEM((frames, patches // CHUNKS, width), jnp.float32),
            low(width, CHUNKS * tokens),
            pltpu.VMEM((dp, block, TILE), jnp.float32),
            low(6, planes, block, third),
            low(4, planes, block, padded),
            low(6, planes - 1, block, third),
            low(4, planes - 1, block, padded),
            low(3, planes, block, third),
            low(3, planes, block, third),
            pltpu.SemaphoreType.DMA((15,)),
            pltpu.SemaphoreType.DMA((7,)),
            pltpu.SemaphoreType.DMA((10,)),
            pltpu.SemaphoreType.DMA((10,)),
            pltpu.SemaphoreType.DMA((10, 4)),
            pltpu.SemaphoreType.DMA((10, 4)),
            pltpu.SemaphoreType.DMA((4,)),
            pltpu.SemaphoreType.DMA((4,)),
            pltpu.SemaphoreType.REGULAR((3,)),
        ],
        compiler_params=pltpu.CompilerParams(
            collective_id=0, has_side_effects=True, vmem_limit_bytes=67043328
        ),
    )(
        latents,
        out_cotangent,
        conditioning,
        clip_mask,
        small,
        qkv_rows,
        proj_weight,
        fc1_weight,
        fc2_weight,
        ada_weight,
    )
    output, grad_latents, grad_cond, qkv_total, qv_total, proj_total = results[:6]
    proj_bias_total, fc1_total, fc1_bias_total, fc2_total, fc2_bias_total, grad_ada, ada_bias_total = results[6:]
    return (
        output,
        grad_latents,
        grad_cond,
        jnp.transpose(qkv_total, (1, 0, 2)),
        qv_total,
        proj_total.T,
        proj_bias_total.reshape(width),
        fc1_total,
        fc1_bias_total.reshape(ff),
        fc2_total.T,
        fc2_bias_total.reshape(width),
        grad_ada,
        ada_bias_total.reshape(-1),
    )


def solution(mesh):
    body = fast_body if fits(mesh) else general_body
    return jax.shard_map(
        body,
        mesh=mesh,
        in_specs=(
            P("dp", None, None, None),
            P("dp", None),
            P("dp"),
            P(None, None, "mp"),
            P(None, "mp"),
            P("mp", None),
            P(),
            P(None, "mp"),
            P("mp"),
            P("mp", None),
            P(),
            P(None, "mp"),
            P("mp"),
            P("dp", None, None, None),
        ),
        out_specs=(
            P("dp", None, None, None),
            P("dp", None, None, None),
            P("dp", None),
            P("dp", None, "mp"),
            P(None, "mp"),
            P("mp", "dp"),
            P(),
            P("dp", "mp"),
            P("mp"),
            P("mp", "dp"),
            P(),
            P("dp", "mp"),
            P("mp"),
        ),
        check_vma=False,
    )
```

```python
from functools import partial

import jax
import jax.numpy as jnp
from jax import lax
from jax.experimental import pallas as pl
from jax.experimental.pallas import tpu as pltpu
from jax.sharding import PartitionSpec as P

HEAD_DIM = 72


def normalize(values):
    centered = values - jnp.mean(values, axis=-1, keepdims=True)
    inverse = lax.rsqrt(jnp.mean(centered * centered, axis=-1, keepdims=True) + 1e-06)
    return (centered * inverse, inverse)


def norm_back(grad_normed, normed, inverse):
    first = jnp.mean(grad_normed, axis=-1, keepdims=True)
    second = jnp.mean(grad_normed * normed, axis=-1, keepdims=True)
    return inverse * (grad_normed - first - normed * second)


def general_body(
    latents,
    conditioning,
    clip_mask,
    qkv_weight,
    qv_bias,
    proj_weight,
    proj_bias,
    fc1_weight,
    fc1_bias,
    fc2_weight,
    fc2_bias,
    ada_weight,
    ada_bias,
    out_cotangent,
):
    frames = latents.shape[1]
    patches = latents.shape[2]
    width = latents.shape[3]
    tok_count = frames * patches
    local_width = qkv_weight.shape[2]
    local_heads = local_width // HEAD_DIM
    factor = HEAD_DIM ** (-0.5)
    stream = latents.reshape(tok_count, width).astype(jnp.float32)
    scaled = jax.nn.silu(conditioning)
    scaled_low = scaled.astype(jnp.bfloat16)
    mod_local = jnp.dot(
        scaled_low, ada_weight, preferred_element_type=jnp.float32
    ) + ada_bias.astype(jnp.float32)
    modulation = lax.all_gather(mod_local, "mp", axis=1, tiled=True).reshape(6, width)
    shift_one = modulation[0]
    scale_one = modulation[1]
    gate_one = modulation[2]
    shift_two = modulation[3]
    scale_two = modulation[4]
    gate_two = modulation[5]
    is_clip = clip_mask[0] > 0
    mask_value = clip_mask[0].astype(jnp.float32)
    normed_one, inverse_one = normalize(stream)
    entry_one = (normed_one * (1.0 + scale_one) + shift_one).astype(jnp.bfloat16)
    qkv_flat = qkv_weight.reshape(width, 3 * local_width)
    bias_rows = qv_bias.astype(jnp.float32)
    bias_full = jnp.stack([bias_rows[0], jnp.zeros_like(bias_rows[0]), bias_rows[1]]).reshape(
        3 * local_width
    )

    def split_heads(projected):
        parts = projected.reshape(frames, patches, 3, local_heads, HEAD_DIM)
        return (parts[:, :, 0], parts[:, :, 1], parts[:, :, 2])

    def softmax_weights(query, keys):
        scores = (
            jnp.einsum("fphd,gphd->phfg", query, keys, preferred_element_type=jnp.float32) * factor
        )
        return jax.nn.softmax(scores, axis=-1)

    def attn_forward(entry):
        projected = (
            jnp.dot(entry, qkv_flat, preferred_element_type=jnp.float32) + bias_full
        ).astype(jnp.bfloat16)
        query, keys, values = split_heads(projected)
        weights = softmax_weights(query, keys)
        mixed = jnp.einsum(
            "phfg,gphd->fphd",
            weights.astype(jnp.bfloat16),
            values,
            preferred_element_type=jnp.float32,
        )
        mixed = mixed.astype(jnp.bfloat16).reshape(tok_count, local_width)
        partial_out = jnp.dot(mixed, proj_weight, preferred_element_type=jnp.float32)
        return (partial_out, projected, mixed)

    def attn_skip(entry):
        return (
            jnp.zeros((tok_count, width), jnp.float32),
            jnp.zeros((tok_count, 3 * local_width), jnp.bfloat16),
            jnp.zeros((tok_count, local_width), jnp.bfloat16),
        )

    partial_out, projected, mixed = lax.cond(is_clip, attn_forward, attn_skip, entry_one)
    attention = lax.psum(partial_out.astype(jnp.bfloat16), "mp").astype(
        jnp.float32
    ) + proj_bias.astype(jnp.float32)
    middle = stream + mask_value * gate_one * attention
    normed_two, inverse_two = normalize(middle)
    entry_two = (normed_two * (1.0 + scale_two) + shift_two).astype(jnp.bfloat16)
    hidden = jnp.dot(entry_two, fc1_weight, preferred_element_type=jnp.float32) + fc1_bias.astype(
        jnp.float32
    )
    activated = jax.nn.gelu(hidden, approximate=True).astype(jnp.bfloat16)
    branch_part = jnp.dot(activated, fc2_weight, preferred_element_type=jnp.float32)
    branch = lax.psum(branch_part.astype(jnp.bfloat16), "mp").astype(jnp.float32) + fc2_bias.astype(
        jnp.float32
    )
    output = middle + gate_two * branch
    grad_out = out_cotangent.reshape(tok_count, width).astype(jnp.float32)
    grad_branch = gate_two * grad_out
    grad_fc2_bias = jnp.sum(grad_branch, axis=0)
    branch_low = grad_branch.astype(jnp.bfloat16)
    grad_fc2 = jnp.einsum("ti,tj->ij", activated, branch_low, preferred_element_type=jnp.float32)
    grad_act = jnp.einsum("tj,ij->ti", branch_low, fc2_weight, preferred_element_type=jnp.float32)
    grad_hidden = jax.vjp(partial(jax.nn.gelu, approximate=True), hidden)[1](grad_act)[0]
    grad_fc1_bias = jnp.sum(grad_hidden, axis=0)
    hidden_low = grad_hidden.astype(jnp.bfloat16)
    grad_fc1 = jnp.einsum("ti,tj->ij", entry_two, hidden_low, preferred_element_type=jnp.float32)
    entry_two_part = jnp.einsum(
        "tj,ij->ti", hidden_low, fc1_weight, preferred_element_type=jnp.float32
    )
    grad_entry_two = lax.psum(entry_two_part.astype(jnp.bfloat16), "mp").astype(jnp.float32)
    grad_gate_two = jnp.sum(grad_out * branch, axis=0)
    grad_shift_two = jnp.sum(grad_entry_two, axis=0)
    grad_scale_two = jnp.sum(grad_entry_two * normed_two, axis=0)
    grad_middle = grad_out + norm_back(grad_entry_two * (1.0 + scale_two), normed_two, inverse_two)
    grad_gate_one = mask_value * jnp.sum(grad_middle * attention, axis=0)
    grad_attention = mask_value * gate_one * grad_middle
    grad_proj_bias = jnp.sum(grad_attention, axis=0)
    attention_low = grad_attention.astype(jnp.bfloat16)

    def attn_backward(operands):
        grad_low, kept_projected, kept_mixed = operands
        grad_proj = jnp.einsum(
            "ti,tj->ij", kept_mixed, grad_low, preferred_element_type=jnp.float32
        )
        grad_mixed = jnp.einsum(
            "tj,ij->ti", grad_low, proj_weight, preferred_element_type=jnp.float32
        )
        grad_mixed = grad_mixed.astype(jnp.bfloat16).reshape(frames, patches, local_heads, HEAD_DIM)
        query, keys, values = split_heads(kept_projected)
        weights = softmax_weights(query, keys)
        grad_values = jnp.einsum(
            "phfg,fphd->gphd",
            weights.astype(jnp.bfloat16),
            grad_mixed,
            preferred_element_type=jnp.float32,
        )
        grad_weights = jnp.einsum(
            "fphd,gphd->phfg", grad_mixed, values, preferred_element_type=jnp.float32
        )
        grad_scores = weights * (
            grad_weights - jnp.sum(weights * grad_weights, axis=-1, keepdims=True)
        )
        grad_scores = grad_scores.astype(jnp.bfloat16)
        grad_query = (
            jnp.einsum("phfg,gphd->fphd", grad_scores, keys, preferred_element_type=jnp.float32)
            * factor
        )
        grad_keys = (
            jnp.einsum("phfg,fphd->gphd", grad_scores, query, preferred_element_type=jnp.float32)
            * factor
        )
        grad_all = (
            jnp.stack([grad_query, grad_keys, grad_values], axis=2)
            .astype(jnp.bfloat16)
            .reshape(tok_count, 3 * local_width)
        )
        column_sums = jnp.sum(grad_all.astype(jnp.float32), axis=0).reshape(3, local_width)
        grad_qv = jnp.stack([column_sums[0], column_sums[2]])
        grad_qkv = jnp.einsum(
            "ti,tj->ij", entry_one, grad_all, preferred_element_type=jnp.float32
        ).reshape(width, 3, local_width)
        grad_entry = jnp.einsum("tj,ij->ti", grad_all, qkv_flat, preferred_element_type=jnp.float32)
        return (grad_proj, grad_qv, grad_qkv, grad_entry)

    def skip_backward(operands):
        return (
            jnp.zeros((local_width, width), jnp.float32),
            jnp.zeros((2, local_width), jnp.float32),
            jnp.zeros((width, 3, local_width), jnp.float32),
            jnp.zeros((tok_count, width), jnp.float32),
        )

    grad_proj, grad_qv, grad_qkv, entry_one_part = lax.cond(
        is_clip, attn_backward, skip_backward, (attention_low, projected, mixed)
    )
    grad_entry_one = lax.psum(entry_one_part.astype(jnp.bfloat16), "mp").astype(jnp.float32)
    grad_shift_one = jnp.sum(grad_entry_one, axis=0)
    grad_scale_one = jnp.sum(grad_entry_one * normed_one, axis=0)
    grad_latents = grad_middle + norm_back(
        grad_entry_one * (1.0 + scale_one), normed_one, inverse_one
    )
    grad_modulation = jnp.concatenate(
        [
            grad_shift_one,
            grad_scale_one,
            grad_gate_one,
            grad_shift_two,
            grad_scale_two,
            grad_gate_two,
        ]
    )
    local_cols = ada_weight.shape[1]
    grad_mod_local = lax.dynamic_slice_in_dim(
        grad_modulation, lax.axis_index("mp") * local_cols, local_cols
    )[None, :]
    grad_ada_bias = jnp.sum(grad_mod_local, axis=0)
    modulation_low = grad_mod_local.astype(jnp.bfloat16)
    scaled_part = jnp.einsum(
        "tj,ij->ti", modulation_low, ada_weight, preferred_element_type=jnp.float32
    )
    grad_scaled = lax.psum(scaled_part, "mp")
    grad_cond = jax.vjp(jax.nn.silu, conditioning)[1](grad_scaled)[0]
    ada_term = jnp.einsum(
        "ti,tj->ij", scaled_low, modulation_low, preferred_element_type=jnp.float32
    )
    grad_ada = lax.psum_scatter(
        ada_term.astype(jnp.bfloat16), "dp", scatter_dimension=0, tiled=True
    ).astype(jnp.float32)
    qkv_total, proj_total, fc1_total, fc2_total = (
        lax.psum_scatter(
            grad_qkv.astype(jnp.bfloat16), "dp", scatter_dimension=0, tiled=True
        ).astype(jnp.float32),
        lax.psum_scatter(
            grad_proj.astype(jnp.bfloat16), "dp", scatter_dimension=1, tiled=True
        ).astype(jnp.float32),
        lax.psum_scatter(
            grad_fc1.astype(jnp.bfloat16), "dp", scatter_dimension=0, tiled=True
        ).astype(jnp.float32),
        lax.psum_scatter(
            grad_fc2.astype(jnp.bfloat16), "dp", scatter_dimension=1, tiled=True
        ).astype(jnp.float32),
    )
    qv_total, proj_bias_total, fc1_bias_total, fc2_bias_total, ada_bias_total = lax.psum(
        (grad_qv, grad_proj_bias, grad_fc1_bias, grad_fc2_bias, grad_ada_bias), "dp"
    )
    return (
        output.reshape(latents.shape),
        grad_latents.reshape(latents.shape),
        grad_cond,
        qkv_total,
        qv_total,
        proj_total,
        proj_bias_total,
        fc1_total,
        fc1_bias_total,
        fc2_total,
        fc2_bias_total,
        grad_ada,
        ada_bias_total,
    )


NT = (((1,), (1,)), ((), ()))
TN = (((0,), (0,)), ((), ()))
CHUNKS = 2
PIECES = 4
TILE = 256
GELU_A = 0.7978845608028654
GELU_B = 0.044715
VMEM = pl.BlockSpec(memory_space=pltpu.VMEM)
ANY = pl.BlockSpec(memory_space=pl.ANY)
ORDERS = ((1, 2, 3), (1, 2, 3), (2, 1, 3), (1, 2, 3), (1, 2, 3), (1, 2, 3), (1, 2, 3), (1, 2, 3), (2, 1, 3), (1, 2, 3))


def f32(values):
    return values.astype(jnp.float32)


def bf16(values):
    return values.astype(jnp.bfloat16)


def dot(left, right, dims=(((1,), (0,)), ((), ()))):
    return lax.dot_general(left, right, dims, preferred_element_type=jnp.float32)


def repeat(count, visit):
    def at(i, carry):
        visit(i)
        return carry

    lax.fori_loop(0, count, at, 0)


def head_spans(width):
    spans = []
    for head in range(width // HEAD_DIM):
        first, last = head * HEAD_DIM, (head + 1) * HEAD_DIM
        low = first // 128 * 128
        high = min(-(-last // 128) * 128, width)
        spans.append((first, last, low, high))
    return spans


def lane_mask(first, last, low, high):
    lane = lax.broadcasted_iota(jnp.int32, (1, high - low), 1) + low
    return (lane >= first) & (lane < last)


def same_patch(tokens, per_frame):
    row = lax.broadcasted_iota(jnp.int32, (tokens, tokens), 0)
    col = lax.broadcasted_iota(jnp.int32, (tokens, tokens), 1)
    return (row % per_frame) == (col % per_frame)


def attention_weights(query, keys, allowed):
    scores = dot(query, keys, NT) * (HEAD_DIM ** (-0.5))
    scores = jnp.where(allowed, scores, -1e30)
    grown = jnp.exp(scores - jnp.max(scores, axis=-1, keepdims=True))
    return grown / jnp.sum(grown, axis=-1, keepdims=True)


def column_blocks(width, block):
    return [(low, min(block, width - low)) for low in range(0, width, block)]


def block_kernel(
    lat_ref,
    dy_ref,
    cond_ref,
    mask_ref,
    small_ref,
    w_hbm,
    pw_hbm,
    w1_hbm,
    w2_hbm,
    ada_hbm,
    out_hbm,
    glat_hbm,
    gcond_ref,
    gqkv_ref,
    gproj_ref,
    rs1_ref,
    rs2_ref,
    gada_ref,
    sums_ref,
    vec_ref,
    stat_ref,
    hsum_ref,
    qsum_ref,
    b1_v,
    modx_v,
    spx_v,
    gath_v,
    wide_v,
    w2_v,
    e1_v,
    proj_v,
    mixed_v,
    e2_v,
    act_v,
    low_v,
    bl_v,
    part1_v,
    recv1_v,
    part2_v,
    recv2_v,
    part3_v,
    recv3_v,
    recv4_v,
    gmid_v,
    stage_v,
    left_v,
    tile_v,
    keep_a,
    keep_b,
    later_a,
    later_b,
    send0_v,
    recv0_v,
    load_sem,
    ada_sem,
    y_send,
    y_recv,
    rs_send,
    rs_recv,
    g_send,
    g_recv,
    credit,
):
    frames, patches, width = lat_ref.shape[1:]
    per_frame = patches // CHUNKS
    tokens = frames * per_frame
    local = proj_v.shape[3]
    padded = mixed_v.shape[2]
    ff = act_v.shape[2]
    planes, rows = send0_v.shape[1], send0_v.shape[2]
    place = lax.axis_index("dp")
    across = 1 - lax.axis_index("mp")
    bit_of = [(place // (1 << b)) % 2 for b in range(4)]
    partner = [place + (1 - 2 * bit_of[b]) * (1 << b) for b in range(4)]
    core = bit_of[0]

    barrier = pltpu.get_barrier_semaphore()
    pl.semaphore_signal(barrier, inc=1, device_id={"mp": across}, device_id_type=pl.DeviceIdType.MESH)
    for other in partner:
        pl.semaphore_signal(barrier, inc=1, device_id={"dp": other}, device_id_type=pl.DeviceIdType.MESH)

    def load(source, target, index):
        copy = pltpu.make_async_copy(source, target, load_sem.at[index])
        copy.start()
        return copy

    def load_attention(index):
        copies = [
            load(w_hbm.at[s], wide_v.at[s * local : (s + 1) * local, :], index + s) for s in range(3)
        ]
        return copies + [load(pw_hbm, wide_v.at[3 * local :, :], index + 3)]

    def load_hidden(index):
        return [
            load(w1_hbm.at[:, i * width : (i + 1) * width], wide_v.at[i * width : (i + 1) * width, :], index + i)
            for i in range(2)
        ]

    deep = act_v.shape[1]
    ada_tail = [
        (low * deep, min(deep, width - low * deep), place_ref)
        for low, place_ref in enumerate(
            (
                act_v.at[0, :, :width],
                act_v.at[0, :, width:],
                act_v.at[1, :, :width],
                act_v.at[1, :, width:],
                low_v.at[0, :, :width],
            )
        )
    ]

    def load_ada():
        pairs = [
            (ada_hbm.at[:, i * width : (i + 1) * width], w2_v.at[i * width : (i + 1) * width, :])
            for i in range(2)
        ]
        for low, size, target in ada_tail:
            pairs.append(
                (ada_hbm.at[low : low + size, 2 * width :], target.at[0:size, :])
            )
        copies = []
        for i, (source, target) in enumerate(pairs):
            copies.append(pltpu.make_async_copy(source, target, ada_sem.at[i]))
            copies[-1].start()
        return copies

    first_ada = load_ada()
    attention_loads = load_attention(0)
    stat_ref[...] = jnp.zeros_like(stat_ref)
    hsum_ref[...] = jnp.zeros_like(hsum_ref)
    for i in range(ff // width):
        b1_v[:, i * width : (i + 1) * width] = small_ref[5 + i : 6 + i, :]
    first_half = lax.axis_index("mp") == 0
    masked = mask_ref[0].astype(jnp.float32)
    SHIFT, PB, B2, B1, QV = 0, 3, 4, 5, 7

    def tall(values):
        return bf16(jnp.broadcast_to(values, (8, values.shape[-1])))

    def modulate():
        sigmoid = 1.0 / (1.0 + jnp.exp(-cond_ref[...]))
        scaled = tall(cond_ref[...] * sigmoid)
        for copy in first_ada:
            copy.wait()
        for i in range(2):
            found = dot(scaled, w2_v[i * width : (i + 1) * width, :])
            modx_v[0, i : i + 1, :] = found[0:1] + small_ref[SHIFT + i : SHIFT + i + 1, :]
        total = small_ref[SHIFT + 2 : SHIFT + 3, :]
        for low, size, target in ada_tail:
            total += dot(scaled[:, low : low + size], target[0:size, :])[0:1]
        modx_v[0, 2:3, :] = total

    def place_modulation():
        def both(i):
            mine, theirs = modx_v[0, i : i + 1, :], modx_v[1, i : i + 1, :]
            return jnp.where(first_half, mine, theirs), jnp.where(first_half, theirs, mine)

        (shift_one, shift_two), (scale_one, scale_two), (gate_one, gate_two) = map(both, range(3))
        vec_ref[0:1, :] = shift_one
        vec_ref[1:2, :] = 1.0 + scale_one
        vec_ref[2:3, :] = masked * gate_one
        vec_ref[3:4, :] = shift_two
        vec_ref[4:5, :] = 1.0 + scale_two
        vec_ref[5:6, :] = gate_two
        vec_ref[6:7, :] = small_ref[PB : PB + 1, :]
        vec_ref[7:8, :] = small_ref[B2 : B2 + 1, :]

    ring = (1, 2, 3, 0)
    slot_bits = [bit_of[b] for b in ring]
    my_slot = sum(v * (1 << i) for i, v in enumerate(slot_bits))

    def vector_rows():
        gath_v[my_slot] = jnp.zeros(gath_v.shape[1:], jnp.float32)
        mine = (stat_ref[4:5, :], stat_ref[5:6, :], masked * stat_ref[2:3, :])
        theirs = (stat_ref[0:1, :], stat_ref[1:2, :], stat_ref[6:7, :])
        for i in range(3):
            gath_v[my_slot, i : i + 1, :] = jnp.where(first_half, mine[i], theirs[i])
        sigmoid = 1.0 / (1.0 + jnp.exp(-cond_ref[...]))
        gath_v[my_slot, 3:4, :] = f32(bf16(cond_ref[...] * sigmoid))
        gath_v[my_slot, 4:5, :] = vec_ref[2:3, :] * stat_ref[3:4, :]
        gath_v[my_slot, 5:6, :] = vec_ref[5:6, :] * stat_ref[7:8, :]
        gath_v[my_slot, 6:7, :] = hsum_ref[:, :width]
        gath_v[my_slot, 7:8, :] = hsum_ref[:, width:]
        gath_v[my_slot, 8:9, :local] = qsum_ref[0:1, :]
        gath_v[my_slot, 9:10, :local] = qsum_ref[2:3, :]

    def gather_step(k):
        held = sum(slot_bits[i] * (1 << i) for i in range(k, 4))
        at = pl.ds(held, 1 << k)
        copy = pltpu.make_async_remote_copy(
            src_ref=gath_v.at[at],
            dst_ref=gath_v.at[at],
            send_sem=g_send.at[k],
            recv_sem=g_recv.at[k],
            device_id={"dp": partner[ring[k]]},
            device_id_type=pl.DeviceIdType.MESH,
        )
        copy.start()
        return copy

    def scaled_back():
        rows_of = [tall(gath_v[my_slot, i : i + 1, :]) for i in range(3)]
        for copy in second_ada:
            copy.wait()
        spx_v[0] = dot(rows_of[0], w2_v[:width, :], NT) + dot(rows_of[1], w2_v[width:, :], NT)
        for low, size, target in ada_tail:
            spx_v[0, :, low : low + size] += dot(rows_of[2], target[0:size, :], NT)

    def conditioning_out():
        total = spx_v[0, 0:1, :] + spx_v[1, 0:1, :]
        cond = cond_ref[...]
        sigmoid = 1.0 / (1.0 + jnp.exp(-cond))
        gcond_ref[...] = total * sigmoid * (1.0 + cond * (1.0 - sigmoid))

    def vectors_out():
        items = gath_v.shape[0]
        total = gath_v[0]
        for i in range(1, items):
            total += gath_v[i]
        sums_ref[...] = total

        def column(row):
            return bf16(jnp.concatenate([gath_v[i, row : row + 1, :] for i in range(items)], axis=0))

        one = lax.broadcasted_iota(jnp.int32, (rows, width), 1)
        down = lax.broadcasted_iota(jnp.int32, (rows, width), 0)
        chosen = jnp.where(one == down + place * rows, 1.0, 0.0).astype(jnp.bfloat16)
        block = bf16(dot(chosen, column(3), NT))
        for i in range(3):
            gada_ref[:, i * width : (i + 1) * width] = dot(block, column(i))

    step = 2 * per_frame

    def token_rows(ref, chunk, i):
        start = chunk * per_frame
        if not isinstance(chunk, int):
            start = pl.multiple_of(start, per_frame)
        block = ref[0, pl.ds(2 * i, 2), pl.ds(start, per_frame), :]
        return f32(block).reshape(step, width)

    def over_rows(visit):
        repeat(tokens // step, lambda i: visit(i, pl.ds(pl.multiple_of(i * step, step), step)))

    def swap(source, target, index, begin=True):
        copy = pltpu.make_async_remote_copy(
            src_ref=source,
            dst_ref=target,
            send_sem=y_send.at[index],
            recv_sem=y_recv.at[index],
            device_id={"mp": across},
            device_id_type=pl.DeviceIdType.MESH,
        )
        if begin:
            copy.start()
        return copy

    def add_stat(row, values):
        stat_ref[row : row + 1, :] += jnp.sum(values, axis=0, keepdims=True)

    def bias_of(s):
        if s == 1:
            return jnp.zeros((1, local), jnp.float32)
        return small_ref[QV + s // 2 : QV + s // 2 + 1, :local]

    allowed = same_patch(tokens, per_frame)
    spans = head_spans(local)
    factor = HEAD_DIM ** (-0.5)

    def first_stage(c):
        def enter(i, at):
            normed, _ = normalize(token_rows(lat_ref, c, i))
            e1_v[c, at, :] = bf16(normed * vec_ref[1:2, :] + vec_ref[0:1, :])

        over_rows(enter)
        for s in range(3):
            pl.when(c == 0)(attention_loads[s].wait)
            weight = wide_v[s * local : (s + 1) * local, :]
            proj_v[c, s] = bf16(dot(e1_v[c], weight, NT) + bias_of(s))
        mixed_v[c, :, padded - 128 :] = jnp.zeros((tokens, 128), jnp.bfloat16)
        for first, last, low, high in spans:
            mask = lane_mask(first, last, low, high)
            query = jnp.where(mask, proj_v[c, 0, :, low:high], 0)
            weights = attention_weights(query, proj_v[c, 1, :, low:high], allowed)
            mixed = dot(bf16(weights), proj_v[c, 2, :, low:high])
            mixed_v[c, :, low:high] = bf16(jnp.where(mask, mixed, f32(mixed_v[c, :, low:high])))
        pl.when(c == 0)(attention_loads[3].wait)
        part1_v[c] = bf16(dot(mixed_v[c, :, :local], wide_v[3 * local :, :]))

    def act_grad_stage(c):
        def enter(i, at):
            grad = token_rows(dy_ref, c, i)
            add_stat(7, grad)
            bl_v[c, at, :] = bf16(grad * vec_ref[5:6, :])

        over_rows(enter)

        def columns(j):
            at = pl.ds(pl.multiple_of(j * TILE, TILE), TILE)
            low_v[c, :, at] = bf16(dot(bl_v[c], w2_v[at, :], NT))

        repeat(ff // TILE, columns)

    def middle_rows(c, i, at):
        attention = f32(part1_v[c, at, :]) + f32(recv1_v[c, at, :]) + vec_ref[6:7, :]
        return attention, token_rows(lat_ref, c, i) + vec_ref[2:3, :] * attention

    def second_stage(c):
        def enter(i, at):
            _, middle = middle_rows(c, i, at)
            normed, _ = normalize(middle)
            e2_v[c, at, :] = bf16(normed * vec_ref[4:5, :] + vec_ref[3:4, :])

        over_rows(enter)

        def half(i):
            base = pl.multiple_of(i * width, width)
            for low, size in column_blocks(width, TILE):
                at = pl.ds(pl.multiple_of(base + low, 128), size)
                hidden = dot(e2_v[c], wide_v[pl.ds(base, width), low : low + size]) + b1_v[:, at]
                square = hidden * hidden
                bent = jnp.tanh(GELU_A * hidden * (1.0 + GELU_B * square))
                gate = 0.5 * (1.0 + bent)
                act_v[c, :, at] = bf16(hidden * gate)
                slope = gate + 0.5 * hidden * (1.0 - bent * bent) * (
                    GELU_A * (1.0 + 3.0 * GELU_B * square)
                )
                grad_hidden = f32(low_v[c, :, at]) * slope
                found = jnp.sum(grad_hidden, axis=0, keepdims=True)
                hsum_ref[:, at] += found
                low_v[c, :, at] = bf16(grad_hidden)

        repeat(ff // width, half)
        for low, size in column_blocks(width, 2 * TILE):
            total = dot(low_v[c, :, :width], wide_v[low : low + size, :], NT)
            total += dot(low_v[c, :, width:], wide_v[width + low : width + low + size, :], NT)
            part3_v[c, :, low : low + size] = bf16(total)

    def branch_stage(c):
        for low, size in column_blocks(width, 2 * TILE):
            part2_v[c, :, low : low + size] = bf16(dot(act_v[c], w2_v[:, low : low + size]))

    def third_stage(c):
        grads = [act_v.at[c, :, s * padded : (s + 1) * padded] for s in range(3)]
        alow = low_v.at[c, :, :width]
        mixed_grad = low_v.at[c, :, width : width + padded]

        def enter(i, at):
            attention, middle = middle_rows(c, i, at)
            normed, inverse = normalize(middle)
            grad_entry = f32(part3_v[c, at, :]) + f32(recv3_v[c, at, :])
            add_stat(0, grad_entry)
            add_stat(1, grad_entry * normed)
            grad_middle = token_rows(dy_ref, c, i) + norm_back(
                grad_entry * vec_ref[4:5, :], normed, inverse
            )
            add_stat(2, grad_middle * attention)
            add_stat(3, grad_middle)
            gmid_v[c, pl.ds(2 * i, 2)] = grad_middle.reshape(2, per_frame, width)
            alow[at, :] = bf16(vec_ref[2:3, :] * grad_middle)

        over_rows(enter)
        if c == 0:
            reloads[3].wait()
        mixed_grad[:, :local] = bf16(dot(alow[...], wide_v[3 * local :, :], NT))
        for first, last, low, high in spans:
            mask = lane_mask(first, last, low, high)
            query, keys, values = (proj_v[c, s, :, low:high] for s in range(3))
            grad_mixed = mixed_grad[:, low:high]
            weights = attention_weights(jnp.where(mask, query, 0), keys, allowed)
            grad_weights = dot(jnp.where(mask, grad_mixed, 0), values, NT)
            grad_scores = bf16(
                weights * (grad_weights - jnp.sum(weights * grad_weights, axis=-1, keepdims=True))
            )
            found = (
                dot(grad_scores, keys) * factor,
                dot(grad_scores, query, TN) * factor,
                dot(bf16(weights), grad_mixed, TN),
            )
            for s in range(3):
                grads[s][:, low:high] = bf16(jnp.where(mask, found[s], f32(grads[s][:, low:high])))
        for s in range(3):
            if c == 0:
                reloads[s].wait()
            found = jnp.sum(f32(grads[s][:, :local]), axis=0, keepdims=True)
            if c == 0:
                qsum_ref[s : s + 1, :] = found
            else:
                qsum_ref[s : s + 1, :] += found
        swaps3[c].wait_send()
        for low, size in column_blocks(width, 2 * TILE):
            at = slice(low, low + size)
            total = dot(grads[0][:, :local], wide_v[:local, at])
            total += dot(grads[1][:, :local], wide_v[local : 2 * local, at])
            total += dot(grads[2][:, :local], wide_v[2 * local : 3 * local, at])
            part3_v[c, :, at] = bf16(total)

    def last_stage(c):
        def leave(i, at):
            normed, inverse = normalize(token_rows(lat_ref, c, i))
            grad_entry = f32(part3_v[c, at, :]) + f32(recv4_v[c, at, :])
            add_stat(4, grad_entry)
            add_stat(5, grad_entry * normed)
            result = norm_back(grad_entry * vec_ref[1:2, :], normed, inverse)
            gmid_v[c, pl.ds(2 * i, 2)] += result.reshape(2, per_frame, width)

        over_rows(leave)
        return load(
            gmid_v.at[c], glat_hbm.at[0, :, c * per_frame : (c + 1) * per_frame, :], 11 + c
        )

    def output_stage(c):
        def leave(i, at):
            _, middle = middle_rows(c, i, at)
            branch = f32(part2_v[c, at, :]) + f32(recv2_v[c, at, :]) + vec_ref[7:8, :]
            add_stat(6, token_rows(dy_ref, c, i) * branch)
            stage_v[pl.ds(2 * i, 2)] = (middle + vec_ref[5:6, :] * branch).reshape(
                2, per_frame, width
            )

        over_rows(leave)
        return load(stage_v, out_hbm.at[0, :, c * per_frame : (c + 1) * per_frame, :], 13 + c)

    third = send0_v.shape[3]
    started = {}

    def unit_refs(u):
        if u < 6:
            return keep_a.at[u], later_a.at[u], third
        return keep_b.at[u - 6], later_b.at[u - 6], padded

    def left_side(source):
        for c in range(CHUNKS):
            left_v[:, c * tokens : (c + 1) * tokens] = source(c).T

    def weight_unit(u, right):
        keep, _, columns = unit_refs(u)
        slot = u % 3
        if u >= 3:
            started[u - 3, 0].wait_send()
        send = send0_v.at[slot]

        def part(low, size):
            block = jnp.concatenate([right(c, low, size) for c in range(CHUNKS)], axis=0)
            half = width // 2
            for i in range(2):
                found = dot(left_v[i * half : (i + 1) * half, :], block)
                tile_v[i * planes : (i + 1) * planes, :, :size] = found.reshape(planes, rows, size)
            first, second, third_bit = ORDERS[u]
            for j in range(planes):
                even = (j // 4 << first) + (j // 2 % 2 << second) + (j % 2 << third_bit)
                keep[j, :, pl.ds(low, size)] = bf16(tile_v[even + core, :, :size])
                send[j, :, pl.ds(low, size)] = bf16(tile_v[even + 1 - core, :, :size])

        if columns % TILE == 0:
            repeat(columns // TILE, lambda t: part(pl.multiple_of(t * TILE, TILE), TILE))
        else:
            whole = columns // TILE
            repeat(whole, lambda t: part(pl.multiple_of(t * TILE, TILE), TILE))
            part(whole * TILE, columns - whole * TILE)
        if u >= 3:
            pl.semaphore_wait(credit.at[slot], 1)
        copy = pltpu.make_async_remote_copy(
            src_ref=send.at[:, :, 0:columns],
            dst_ref=recv0_v.at[slot, :, :, 0:columns],
            send_sem=rs_send.at[u, 0],
            recv_sem=rs_recv.at[u, 0],
            device_id={"dp": partner[0]},
            device_id_type=pl.DeviceIdType.MESH,
        )
        copy.start()
        started[u, 0] = copy

    def advance(u, stage):
        keep, later, columns = unit_refs(u)
        slot = u % 3
        order = ORDERS[u]
        started[u, stage - 1].wait_recv()
        base = sum(bit_of[order[i]] * (4 >> i) for i in range(stage - 1))
        if stage == 1:
            come = recv0_v.at[slot, :, :, 0:columns]
        else:
            come = later.at[(0, 4, 6)[stage - 2] :]
        if stage == 4:
            total = f32(keep[base]) + f32(come[0])
            if u < 3:
                rs2_ref[:, u * third : (u + 1) * third] = total
            elif u < 6:
                rs1_ref[:, (u - 3) * third : (u - 2) * third] = total
            elif u < 9:
                gqkv_ref[u - 6] = total[:, :local]
            else:
                gproj_ref[...] = total[:, :local]
            return
        count = 4 >> (stage - 1)
        mine = bit_of[order[stage - 1]]

        def add(which):
            def one(i):
                at = which * count + i
                keep[base + at] = bf16(f32(keep[base + at]) + f32(come[at]))

            repeat(count, one)

        add(1 - mine)
        other = partner[order[stage - 1]]
        copy = pltpu.make_async_remote_copy(
            src_ref=keep.at[pl.ds(base + (1 - mine) * count, count)],
            dst_ref=later.at[(0, 4, 6)[stage - 1] : (0, 4, 6)[stage - 1] + count],
            send_sem=rs_send.at[u, stage],
            recv_sem=rs_recv.at[u, stage],
            device_id={"dp": other},
            device_id_type=pl.DeviceIdType.MESH,
        )
        copy.start()
        started[u, stage] = copy
        add(mine)
        if stage == 1 and u < 7:
            pl.semaphore_signal(
                credit.at[slot],
                inc=1,
                device_id={"dp": partner[0]},
                device_id_type=pl.DeviceIdType.MESH,
            )

    def hidden_unit(u, right_v):
        weight_unit(u, lambda c, low, size: right_v[c, :, pl.ds((u % 3) * third + low, size)])

    modulate()
    pl.semaphore_wait(barrier, 5)
    mod_swap = swap(modx_v.at[0], modx_v.at[1], 8)
    w2_load = load(w2_hbm, w2_v, 4)
    mod_swap.wait_recv()
    place_modulation()
    def first_swap(c, begin=True):
        return swap(part1_v.at[c], recv1_v.at[c], c, begin)

    def third_swap(c, begin=True):
        return swap(part3_v.at[c], recv3_v.at[c], 2 + c, begin)

    def first_step(c):
        first_stage(c)
        first_swap(c)

    def second_step(c):
        first_swap(c, False).wait_recv()
        second_stage(c)
        third_swap(c)

    repeat(CHUNKS, first_step)
    hidden_loads = load_hidden(5)
    w2_load.wait()
    repeat(CHUNKS, act_grad_stage)
    for copy in hidden_loads:
        copy.wait()
    repeat(CHUNKS, second_step)
    swaps1 = [first_swap(c, False) for c in range(CHUNKS)]
    swaps3 = [third_swap(c, False) for c in range(CHUNKS)]
    reloads = load_attention(7)
    left_side(lambda c: bl_v[c])
    for u in range(3):
        hidden_unit(u, act_v)
    advance(0, 1)
    left_side(lambda c: e2_v[c])
    hidden_unit(3, low_v)
    advance(1, 1)
    hidden_unit(4, low_v)
    advance(2, 1)
    hidden_unit(5, low_v)
    repeat(CHUNKS, branch_stage)
    swaps3[0].wait_recv()
    advance(0, 2)
    third_stage(0)
    swaps4 = [swap(part3_v.at[0], recv4_v.at[0], 6)]
    advance(3, 1)
    advance(1, 2)
    advance(2, 2)
    swaps3[1].wait_recv()
    third_stage(1)
    swaps4.append(swap(part3_v.at[1], recv4_v.at[1], 7))
    swaps2 = [swap(part2_v.at[c], recv2_v.at[c], 4 + c) for c in range(CHUNKS)]
    advance(4, 1)
    advance(0, 3)
    advance(1, 3)
    advance(2, 3)
    advance(3, 2)
    left_side(lambda c: e1_v[c])
    for s in range(3):
        weight_unit(
            6 + s, lambda c, low, size, s=s: act_v[c, :, pl.ds(s * padded + low, size)]
        )
        if s == 0:
            advance(5, 1)
            advance(4, 2)
            advance(0, 4)
            advance(1, 4)
        elif s == 1:
            advance(6, 1)
            advance(2, 4)
    left_side(lambda c: low_v[c, :, :width])
    advance(5, 2)
    weight_unit(9, lambda c, low, size: mixed_v[c, :, pl.ds(low, size)])
    advance(7, 1)
    advance(3, 3)
    swaps2[0].wait_recv()
    writes = [output_stage(0)]
    advance(8, 1)
    advance(4, 3)
    advance(9, 1)
    swaps4[0].wait_recv()
    writes.append(last_stage(0))
    advance(5, 3)
    advance(3, 4)
    writes[0].wait()
    swaps2[1].wait_recv()
    writes.append(output_stage(1))
    swaps4[1].wait_recv()
    writes.append(last_stage(1))
    second_ada = load_ada()
    vector_rows()
    gathers = [gather_step(0)]
    advance(4, 4)
    advance(6, 2)
    scaled_back()
    scaled_swap = swap(spx_v.at[0], spx_v.at[1], 9)
    advance(5, 4)
    gathers[0].wait_recv()
    gathers.append(gather_step(1))
    advance(8, 2)
    advance(7, 2)
    advance(6, 3)
    gathers[1].wait_recv()
    gathers.append(gather_step(2))
    advance(8, 3)
    advance(7, 3)
    advance(9, 2)
    gathers[2].wait_recv()
    gathers.append(gather_step(3))
    scaled_swap.wait_recv()
    conditioning_out()
    advance(6, 4)
    advance(8, 4)
    gathers[3].wait_recv()
    vectors_out()
    advance(9, 3)
    advance(7, 4)
    advance(9, 4)
    for copy in writes[1:]:
        copy.wait()
    for copy in swaps1 + swaps2 + swaps4 + [mod_swap, scaled_swap] + gathers:
        copy.wait_send()
    for (u, stage), copy in started.items():
        if stage > 0 or u >= 7:
            copy.wait_send()


def finish_kernel(*refs):
    count = (len(refs) - 10) // 3
    sources, (cond_ref, sums_ref) = refs[:count], refs[count : count + 2]
    targets, outs = refs[count + 2 : 2 * count + 2], refs[2 * count + 2 : 2 * count + 8]
    held, (in_sem, out_sem) = refs[2 * count + 8 : 3 * count + 8], refs[3 * count + 8 :]
    pairs = []
    for i in range(count):
        pieces = PIECES if len(sources[i].shape) == 4 else 1
        size = sources[i].shape[1] // pieces
        for p in range(pieces):
            at = pl.ds(p * size, size)
            ways = [ref.at[:, at] if pieces > 1 else ref for ref in (sources[i], held[i], targets[i])]
            first = pltpu.make_async_copy(ways[0], ways[1], in_sem.at[i, p])
            second = pltpu.make_async_copy(ways[1], ways[2], out_sem.at[i, p])
            first.start()
            pairs.append((first, second))
    gcond_ref, gqv_ref, gpb_ref, gb1_ref, gb2_ref, gadab_ref = outs
    width = gpb_ref.shape[0]
    gcond_ref[...] = cond_ref[...]
    gqv_ref[...] = sums_ref[8:10, : gqv_ref.shape[1]]
    gpb_ref[...] = sums_ref[4, :]
    gb2_ref[...] = sums_ref[5, :]
    for i in range(2):
        gb1_ref[i * width : (i + 1) * width] = sums_ref[6 + i, :]
    for i in range(3):
        gadab_ref[i * width : (i + 1) * width] = sums_ref[i, :]
    for first, second in pairs:
        first.wait()
        second.start()
    for _, second in pairs:
        second.wait()


def fits(mesh):
    return mesh.shape["mp"] == 2 and mesh.shape["dp"] == 16


def fast_body(
    latents,
    conditioning,
    clip_mask,
    qkv_weight,
    qv_bias,
    proj_weight,
    proj_bias,
    fc1_weight,
    fc1_bias,
    fc2_weight,
    fc2_bias,
    ada_weight,
    ada_bias,
    out_cotangent,
):
    frames, patches, width = latents.shape[1:]
    local = qkv_weight.shape[2]
    padded = -(-local // 128) * 128
    ff = fc1_weight.shape[1]
    dp = lax.axis_size("dp")
    tokens = frames * patches // CHUNKS
    block = width // dp

    wide = [ada_bias, proj_bias, fc2_bias, fc1_bias, qv_bias[0], qv_bias[1]]
    starts = (0, 3 * width, 4 * width, 5 * width, 5 * width + ff, 6 * width + ff)
    total = 7 * width + ff
    small = sum(
        jnp.pad(f32(part), (start, total - start - part.shape[0])) for part, start in zip(wide, starts)
    ).reshape(-1, width)
    qkv_rows = jnp.transpose(qkv_weight, (1, 2, 0))

    def struct(*shape, dtype=jnp.float32):
        return jax.ShapeDtypeStruct(shape, dtype)

    def low(*shape):
        return pltpu.VMEM(shape, jnp.bfloat16)

    planes, third = dp // 2, ff // 3
    outs = [
        (struct(*latents.shape), ANY),
        (struct(*latents.shape), ANY),
        (struct(1, width), VMEM),
        (struct(3, block, local), VMEM),
        (struct(block, local), VMEM),
        (struct(block, ff), VMEM),
        (struct(block, ff), VMEM),
        (struct(block, 3 * width), VMEM),
        (struct(10, width), VMEM),
    ]
    by_token = low(CHUNKS, tokens, width)
    results = pl.pallas_call(
        block_kernel,
        in_specs=[VMEM] * 3 + [pl.BlockSpec(memory_space=pltpu.SMEM), VMEM] + [ANY] * 5,
        out_specs=[spec for _, spec in outs],
        out_shape=[shape for shape, _ in outs],
        scratch_shapes=[
            pltpu.VMEM((8, width), jnp.float32),
            pltpu.VMEM((8, width), jnp.float32),
            pltpu.VMEM((1, ff), jnp.float32),
            pltpu.VMEM((3, local), jnp.float32),
            pltpu.VMEM((1, ff), jnp.float32),
            pltpu.VMEM((2, 8, width), jnp.float32),
            pltpu.VMEM((2, 8, width), jnp.float32),
            pltpu.VMEM((dp, 10, width), jnp.float32),
            low(4 * local, width),
            low(ff, width),
            by_token,
            low(CHUNKS, 3, tokens, local),
            low(CHUNKS, tokens, padded),
            by_token,
            low(CHUNKS, tokens, ff),
            low(CHUNKS, tokens, ff),
            by_token,
            *[by_token] * 7,
            pltpu.VMEM((CHUNKS, frames, patches // CHUNKS, width), jnp.float32),
            pltpu.VMEM((frames, patches // CHUNKS, width), jnp.float32),
            low(width, CHUNKS * tokens),
            pltpu.VMEM((dp, block, TILE), jnp.float32),
            low(6, planes, block, third),
            low(4, planes, block, padded),
            low(6, planes - 1, block, third),
            low(4, planes - 1, block, padded),
            low(3, planes, block, third),
            low(3, planes, block, third),
            pltpu.SemaphoreType.DMA((15,)),
            pltpu.SemaphoreType.DMA((7,)),
            pltpu.SemaphoreType.DMA((10,)),
            pltpu.SemaphoreType.DMA((10,)),
            pltpu.SemaphoreType.DMA((10, 4)),
            pltpu.SemaphoreType.DMA((10, 4)),
            pltpu.SemaphoreType.DMA((4,)),
            pltpu.SemaphoreType.DMA((4,)),
            pltpu.SemaphoreType.REGULAR((3,)),
        ],
        compiler_params=pltpu.CompilerParams(
            collective_id=0, has_side_effects=True, vmem_limit_bytes=67043328
        ),
    )(
        latents,
        out_cotangent,
        conditioning,
        clip_mask,
        small,
        qkv_rows,
        proj_weight,
        fc1_weight,
        fc2_weight,
        ada_weight,
    )
    moved = results[:2] + results[5:8] + results[3:5]
    flat = [struct(width), struct(ff), struct(width), struct(3 * width)]
    same = [struct(*array.shape) for array in moved]
    finished = pl.pallas_call(
        finish_kernel,
        in_specs=[ANY] * len(moved) + [VMEM] * 2,
        out_specs=[ANY] * len(moved) + [VMEM] * 6,
        out_shape=same + [struct(1, width), struct(2, local)] + flat,
        scratch_shapes=[
            *[pltpu.VMEM(array.shape, jnp.float32) for array in moved],
            pltpu.SemaphoreType.DMA((len(moved), PIECES)),
            pltpu.SemaphoreType.DMA((len(moved), PIECES)),
        ],
    )(*moved, results[2], results[8])
    output, grad_latents, fc1_total, fc2_total, grad_ada, qkv_total, proj_total = finished[:7]
    grad_cond, qv_total, proj_bias_total, fc1_bias_total, fc2_bias_total, ada_bias_total = finished[7:]
    return (
        output,
        grad_latents,
        grad_cond,
        jnp.transpose(qkv_total, (1, 0, 2)),
        qv_total,
        proj_total.T,
        proj_bias_total,
        fc1_total,
        fc1_bias_total,
        fc2_total.T,
        fc2_bias_total,
        grad_ada,
        ada_bias_total,
    )


def solution(mesh):
    body = fast_body if fits(mesh) else general_body
    return jax.shard_map(
        body,
        mesh=mesh,
        in_specs=(
            P("dp", None, None, None),
            P("dp", None),
            P("dp"),
            P(None, None, "mp"),
            P(None, "mp"),
            P("mp", None),
            P(),
            P(None, "mp"),
            P("mp"),
            P("mp", None),
            P(),
            P(None, "mp"),
            P("mp"),
            P("dp", None, None, None),
        ),
        out_specs=(
            P("dp", None, None, None),
            P("dp", None, None, None),
            P("dp", None),
            P("dp", None, "mp"),
            P(None, "mp"),
            P("mp", "dp"),
            P(),
            P("dp", "mp"),
            P("mp"),
            P("mp", "dp"),
            P(),
            P("dp", "mp"),
            P("mp"),
        ),
        check_vma=False,
    )
```
